256 devices in a mesh: grid: 64 (over z, y, core), lev: 4 (over x).
Axes of the slice: x: 4, y: 4, z: 8, core: 2. Of those that a mesh axis runs over, the one named last changes fastest.
Arguments:
- prior_fields: float32 [128, 8, 32768], P('grid', 'lev'), may hold values from -6 to 6
- channel_weights: float32 [8, 4], P('lev'), may hold values from 0.1 to 1
- obs_owner: int32 [4], replicated, may hold values from 0 to 63
- obs_offset: int32 [4, 4, 64], replicated, may hold values from 0 to 511
- obs_value: float32 [4, 4, 64], P(None, 'lev'), may hold values from -30 to 30
- obs_error: float32 [4, 4, 64], P(None, 'lev'), may hold values from 0.5 to 2
- ancestors: int32 [4, 4, 64, 128], P(None, 'lev', 'grid'), may hold values from 0 to 127
Outputs:
- posterior_fields: float32 [128, 8, 32768], P('grid', 'lev')
The draws below stay inside these ranges and needn't reach their ends.
All inputs are finite; a program needn't handle non-finite values.
Results may differ from the reference program's by a relative error of at most 0.0003.
Values sent between devices are 32-bit elements; how exact they have to be, the bound alone decides.
A program may use at most 128 MiB of HBM per device.

```python
import math
import jax
import jax.numpy as jnp
from jax import lax

M = 128
CELLS_DEV = 512
OBS = 64
NB = 4
BLOCKS = 64
GROUPS = 4
LEVELS = 8
CELLS = 32768
REGIONS = 64
N_GRID = 64


def draw_obs_value(key, part):
    base = jax.random.normal(key, (NB, GROUPS, OBS), jnp.float32)
    return jnp.clip(1.5 * base, -30.0, 30.0)


def with_ends(values, stream_key, smallest, largest):
    extent = values.shape
    place = [jax.random.randint(jax.random.fold_in(stream_key, axis), (), 0, extent[axis]) for axis in range(len(extent))]
    values = values.at[tuple(place)].set(smallest)
    longest = extent.index(max(extent))
    place[longest] = (place[longest] + 1) % extent[longest]
    return values.at[tuple(place)].set(largest)


def block_levels(stream_key, dims, shards, smallest, high):
    gain = 1.0
    for position, blocks in shards:
        draws = jax.random.uniform(jax.random.fold_in(jax.random.fold_in(stream_key, 6), position), (blocks,), jnp.float32, smallest / len(shards), high / len(shards))
        gain = gain * jnp.repeat(jnp.exp(draws), dims[position] // blocks).reshape((-1,) + (1,) * (len(dims) - 1 - position))
    return gain


def noise(key, extent, deviation, most, cuts=(), held_as=jnp.bfloat16):
    result = deviation * jax.random.normal(key, extent, jnp.float32)
    if cuts:
        result = result * block_levels(key, extent, cuts, -0.22, 0.18)
    return jnp.clip(result, -most, most).astype(held_as)


def setup_inputs(seed: int = 0) -> dict:
    streams_of = jax.random.split(jax.random.key(seed), 8)
    prior_fields = noise(streams_of[0], (M, LEVELS, CELLS), 1.0, 6.0, ((0, 64), (1, 4)), jnp.float32)
    channel_weights = jnp.clip(0.1 + 0.9 * jax.random.uniform(streams_of[1], (LEVELS, GROUPS), jnp.float32) ** block_levels(streams_of[1], (LEVELS, GROUPS), ((0, 4),), -0.2, 0.2), 0.1, 1.0)
    obs_owner = with_ends(jax.random.randint(streams_of[2], (NB,), 0, BLOCKS), jax.random.fold_in(streams_of[2], 1), 0, BLOCKS - 1).astype(jnp.int32)
    obs_offset = with_ends(jax.random.randint(streams_of[3], (NB, GROUPS, OBS), 0, CELLS_DEV), jax.random.fold_in(streams_of[3], 1), 0, CELLS_DEV - 1).astype(jnp.int32)
    obs_value = draw_obs_value(jax.random.fold_in(streams_of[7], 71), 0)
    obs_error = jnp.clip(jnp.exp(math.log(2.0) - 1.3862944 * jax.random.uniform(streams_of[5], (NB, GROUPS, OBS), jnp.float32) ** block_levels(streams_of[5], (NB, GROUPS, OBS), ((1, 4),), -0.2, 0.2)), 0.5, 2.0)
    ancestors = with_ends(jax.random.randint(streams_of[6], (NB, GROUPS, REGIONS, M), 0, M), jax.random.fold_in(streams_of[6], 1), 0, M - 1).astype(jnp.int32)
    return dict(prior_fields=prior_fields, channel_weights=channel_weights, obs_owner=obs_owner, obs_offset=obs_offset, obs_value=obs_value, obs_error=obs_error, ancestors=ancestors)


HIGH = lax.Precision.HIGHEST


def blend_matrices(prior_obs, observed, obs_dev, centres, positions, scale, parents):
    count = observed.shape[0]
    members = prior_obs.shape[1]
    innovation = ((observed[:, None] - prior_obs) / obs_dev[:, None]) ** 2
    distance = (centres[:, None] - positions[None, :]) / scale
    taper = jnp.exp(-0.5 * distance * distance)
    log_weight = (-0.5 / count) * jnp.dot(taper, innovation, precision=HIGH)
    top_value = jnp.max(log_weight, axis=1, keepdims=True)
    expo_weight = jnp.exp(log_weight - top_value)
    weight = expo_weight / jnp.sum(expo_weight, axis=1, keepdims=True)
    alpha = 0.8 * (1.0 - jnp.exp(-jnp.sum(taper, axis=1) / count))
    onehot = (parents[:, :, None] == jnp.arange(members, dtype=jnp.int32)[None, None, :]).astype(jnp.float32)
    identity = jnp.eye(members, dtype=jnp.float32)
    remain = 1.0 - alpha
    return alpha[:, None, None] * onehot + remain[:, None, None] * identity[None] + (weight - 1.0 / members)[:, None, :]


def reference(prior_fields, channel_weights, obs_owner, obs_offset, obs_value, obs_error, ancestors):
    members, levels, cells = prior_fields.shape
    groups = channel_weights.shape[1]
    group_depth = levels // groups
    regions = ancestors.shape[2]
    region_cells = cells // regions
    block_cells = cells // N_GRID
    scale = regions / 2.0
    centres = jnp.arange(regions, dtype=jnp.int32).astype(jnp.float32) + 0.5
    fields = prior_fields
    for batch in range(NB):
        obs_cells = (obs_owner[batch] * block_cells + obs_offset[batch]).astype(jnp.int32)
        picked = fields[:, :, obs_cells.reshape(-1)].reshape(members, levels, groups, OBS)
        priors = jnp.einsum("mlgk,lg->gkm", picked, channel_weights, precision=HIGH)
        pieces = []
        for group in range(groups):
            positions = obs_cells[group].astype(jnp.float32) / region_cells
            blend = blend_matrices(priors[group], obs_value[batch, group], obs_error[batch, group], centres, positions, scale, ancestors[batch, group])
            slab = fields[:, group * group_depth:(group + 1) * group_depth, :].reshape(members, group_depth, regions, region_cells)
            mixed = jnp.einsum("rjm,mlrc->jlrc", blend, slab, precision=HIGH)
            pieces.append(mixed.reshape(members, group_depth, cells))
        fields = jnp.concatenate(pieces, axis=1)
    return fields
```

```python
import functools

import jax
import jax.numpy as jnp
from jax import lax
from jax.experimental import pallas as pl
from jax.experimental.pallas import tpu as pltpu
from jax.sharding import PartitionSpec as P

NB = 4
LANES = 128
F32 = jnp.float32
BF16 = jnp.bfloat16
MESH = pl.DeviceIdType.MESH
PAIRS = [(1, 0), (2, 0), (2, 1), (3, 0), (3, 1), (3, 2)]


def iota(shape, axis):
    return lax.broadcasted_iota(jnp.int32, shape, axis)


def split3(v):
    hi = v.astype(BF16)
    rest = v - hi.astype(F32)
    mid = rest.astype(BF16)
    low = (rest - mid.astype(F32)).astype(BF16)
    return hi, mid, low


def dot(a, b):
    return jnp.dot(a, b, preferred_element_type=F32)


def pick_dot(onehot, v):
    hi, mid, low = split3(v)
    return (dot(onehot, low) + dot(onehot, mid)) + dot(onehot, hi)


def kernel(
    n_grid, n_lev, owner, cw, x, off, val, err, anc, out,
    pay, gath, f, y, ys, ssend, srecv, csend, crecv,
    z_sem, y_sem, c_sem, in_sem, out_sem, s_sem, r_sem,
):
    slab = x.shape[0]
    rows = x.shape[1] // n_grid
    members = slab * n_grid
    count = off.shape[2]
    block = rows * LANES // 2
    n_core, n_y = 2, 4
    n_z = n_grid // (n_core * n_y)
    scale = n_grid / 2.0
    per = 12
    prow = per * slab

    me = lax.axis_index("grid")
    lev = lax.axis_index("lev")
    core = me % n_core
    yy = (me // n_core) % n_y
    zz = me // (n_core * n_y)

    def slot_of(g):
        return (g % n_core) * (n_y * n_z) + ((g // n_core) % n_y) * n_z + g // (n_core * n_y)

    def grid_of(s):
        return ((s % n_z) * n_y + (s // n_z) % n_y) * n_core + s // (n_z * n_y)

    my_slot = slot_of(me)

    def send(src, dst, sem, grid, level):
        pltpu.make_async_remote_copy(
            src_ref=src, dst_ref=dst, send_sem=sem.at[0], recv_sem=sem.at[1],
            device_id=(grid, level), device_id_type=MESH,
        ).start()

    def drain(ref, sem):
        pltpu.make_async_copy(ref, ref, sem).wait()

    lane256 = iota((1, n_lev * count), 1)
    wrow = []
    for level in range(2):
        w = jnp.zeros((1, n_lev * count), F32)
        for g in range(n_lev):
            w = jnp.where(lane256 // count == g, cw[level, g], w)
        wrow.append(w)
    row16 = iota((slab * rows, n_lev * count), 0)
    weights = jnp.where(row16 % 2 == 0, wrow[0], wrow[1])
    tile_of_row = (row16 % rows) // 2
    pay[...] = jnp.zeros_like(pay)

    def scan_blocks(k, tiles):
        tile = x[:, pl.ds(pl.multiple_of(k * rows, rows), rows), :]
        return tuple(jnp.where(owner[b] == k, tile, kept) for b, kept in enumerate(tiles))

    zero = jnp.zeros((slab, rows, LANES), F32)
    tiles = lax.fori_loop(0, n_grid, scan_blocks, (zero,) * NB, unroll=8)
    for b in range(NB):
        src = tiles[b].reshape(slab * rows, LANES)
        cells = jnp.concatenate([off[b, g : g + 1, :] for g in range(n_lev)], axis=1)
        onehot = (iota((LANES, n_lev * count), 0) == cells % LANES).astype(BF16)
        hi, mid, low = split3(src)
        got = (dot(low, onehot) + dot(mid, onehot)) + dot(hi, onehot)
        got = jnp.where(tile_of_row == cells // LANES, got * weights, 0.0)
        for i in range(slab):
            value = jnp.sum(got[i * rows : (i + 1) * rows], axis=0, keepdims=True)
            for h in range(2):
                pay[i * per + b * 2 + h : i * per + b * 2 + h + 1, :] = value[:, h * LANES : (h + 1) * LANES]
        pay[2 * NB + b : 2 * NB + b + 1, :] = anc[b].astype(F32)

    my_rows = gath.at[pl.ds(pl.multiple_of(my_slot * prow, 8), prow), :]
    for d in range(1, n_z):
        peer = (((zz + d) % n_z) * n_y + yy) * n_core + core
        send(pay, my_rows, z_sem, peer, lev)
    gath[pl.ds(pl.multiple_of(my_slot * prow, 8), prow), :] = pay[...]

    def push_in(t, carry):
        peer = (me + t) % n_grid
        send(
            x.at[:, pl.ds(pl.multiple_of(peer * rows, rows), rows), :],
            f.at[pl.ds(my_slot * slab, slab)],
            in_sem, peer, lev,
        )
        return carry

    lax.fori_loop(1, n_grid, push_in, 0)
    f[pl.ds(my_slot * slab, slab)] = x[:, pl.ds(pl.multiple_of(me * rows, rows), rows), :]

    drain(gath.at[pl.ds(0, (n_z - 1) * prow), :], z_sem.at[1])
    col_rows = gath.at[pl.ds(pl.multiple_of((core * n_y + yy) * n_z * prow, 8), n_z * prow), :]
    for d in range(1, n_y):
        peer = (zz * n_y + (yy + d) % n_y) * n_core + core
        send(col_rows, col_rows, y_sem, peer, lev)

    lane1 = iota((1, LANES), 1)
    member_row = iota((members, LANES), 0)
    member_lane = iota((members, members), 1)
    eye = (iota((members, members), 0) == member_lane).astype(F32)

    taper = {}
    alpha = {}
    for b in range(NB):
        cells = off[b, pl.ds(lev, 1), :]
        where = (owner[b] * block + cells).astype(F32) / block
        where = jnp.concatenate([where, where], axis=1)
        regions = {0: me}
        for later in range(b + 1, NB):
            regions[later] = owner[later]
        for key, region in regions.items():
            distance = ((region.astype(F32) + 0.5) - where) / scale
            t = jnp.exp(-0.5 * distance * distance)
            taper[b, key] = t
            total = jnp.sum(t, axis=1, keepdims=True)
            alpha[b, key] = 0.8 * (1.0 - jnp.exp(-total / (2 * count)))

    perm = (grid_of(iota((members, members), 0) // slab) * slab + iota((members, members), 0) % slab == member_lane).astype(BF16)

    def columns(stack):
        stack = stack.astype(jnp.int32)
        stack = (slot_of(stack // slab) * slab + stack % slab).astype(F32).astype(BF16)
        return lax.dot_general(perm, stack, (((1,), (1,)), ((), ())), preferred_element_type=F32)

    def picker(cols, k):
        return (cols[:, k : k + 1].astype(jnp.int32) == member_lane).astype(BF16)

    own_cols = columns(pay[8:16, :])
    chain = [eye]
    for b in range(NB):
        a = alpha[b, 0]
        chosen = picker(own_cols, b)
        moved = chosen.astype(F32) if b == 0 else pick_dot(chosen, chain[b])
        chain.append(a * moved + (1.0 - a) * chain[b])

    drain(gath.at[pl.ds(0, (n_y - 1) * n_z * prow), :], y_sem.at[1])
    half = n_y * n_z * prow
    core_rows = gath.at[pl.ds(pl.multiple_of(core * half, 8), half), :]
    send(core_rows, core_rows, c_sem, me + 1 - 2 * core, lev)
    drain(gath.at[pl.ds(0, half), :], c_sem.at[1])

    low_half = iota((members // 2, LANES), 1) < count
    slot_row = iota((n_grid, LANES), 0)
    all_parents = [gath[pl.ds(2 * NB + i, n_grid, stride=prow), :] for i in range(NB - 1)]
    found = [
        jnp.sum(jnp.where(slot_row == slot_of(owner[b]), all_parents[i], 0.0), axis=0, keepdims=True)
        for b, i in PAIRS
    ]
    pair_cols = columns(jnp.concatenate(found + found[:2], axis=0))

    def exchange_base(b, v):
        top, bottom = v[: members // 2], v[members // 2 :]
        for g in range(n_lev):
            lanes = slice((g // 2) * LANES, (g // 2 + 1) * LANES)
            a, c = top[:, lanes], bottom[:, lanes]
            if g % 2 == 0:
                packed = jnp.where(low_half, a, pltpu.roll(c, count, 1))
            else:
                packed = jnp.where(low_half, pltpu.roll(a, count, 1), c)
            ssend[b, g] = packed
        for d in range(1, n_lev):
            level = (lev + d) % n_lev
            send(ssend.at[b, level], srecv.at[b, d - 1], s_sem.at[b], me, level)

    for b in range(NB):
        parts = [gath[pl.ds(b * 2 + h, members, stride=per), :] for h in range(2)]
        v = jnp.concatenate(parts, axis=1)
        for i in range(b):
            ys[PAIRS.index((b, i))] = v
            a = alpha[i, b]
            v = a * pick_dot(picker(pair_cols, PAIRS.index((b, i))), v) + (1.0 - a) * v
        exchange_base(b, v)

    shift = {b: jnp.zeros((1, n_lev * count), F32) for b in range(1, NB)}
    mean_row = jnp.zeros((1, members), F32)
    for b in range(NB):
        drain(srecv.at[b], s_sem.at[b, 1])
        prior = ssend[b, lev]
        for d in range(n_lev - 1):
            prior = prior + srecv[b, d]
        if b > 0:
            for g in range(n_lev):
                row = shift[b][:, (g // 2) * LANES : (g // 2 + 1) * LANES]
                other = pltpu.roll(row, count, 1)
                first = lane1 < count
                row = jnp.where(first, row, other) if g % 2 == 0 else jnp.where(first, other, row)
                csend[b - 1, g] = jnp.broadcast_to(row, (8, LANES))
            for d in range(1, n_lev):
                level = (lev + d) % n_lev
                send(csend.at[b - 1, level], crecv.at[b - 1, d - 1], r_sem.at[b - 1], me, level)
            drain(crecv.at[b - 1], r_sem.at[b - 1, 1])
            row = csend[b - 1, lev]
            for d in range(n_lev - 1):
                row = row + crecv[b - 1, d]
            prior = prior + row[0:1, :]
        seen = jnp.concatenate([val[b], val[b]], axis=1)
        dev = jnp.concatenate([err[b], err[b]], axis=1)
        innovation = ((seen - prior) / dev) ** 2
        for key in [0] + list(range(b + 1, NB)):
            weighted = innovation * taper[b, key]
            top = jnp.sum(jnp.where(low_half, weighted, 0.0), axis=1, keepdims=True)
            bottom = jnp.sum(jnp.where(low_half, 0.0, weighted), axis=1, keepdims=True)
            log_weight = (-0.5 / count) * jnp.concatenate([top, bottom], axis=0)
            expo = jnp.exp(log_weight - jnp.max(log_weight, axis=0, keepdims=True))
            change = expo / jnp.sum(expo, axis=0, keepdims=True) - 1.0 / members
            if key == 0:
                mean_row = mean_row + jnp.sum(change * chain[b], axis=0, keepdims=True)
            else:
                shift[key] = shift[key] + jnp.sum(change * ys[PAIRS.index((key, b))], axis=0, keepdims=True)

    total = chain[NB] + mean_row
    t_hi, t_mid, t_low = split3(total)
    drain(f.at[pl.ds(0, members - slab)], in_sem.at[1])
    f2 = f.reshape(members * rows, LANES)
    y2 = y.reshape(members * rows, LANES)
    for s in range(rows):
        hi, mid, low = split3(f2[pl.ds(s, members, stride=rows), :])
        mixed = (dot(t_low, hi) + dot(t_mid, mid)) + dot(t_hi, low)
        mixed = mixed + (dot(t_mid, hi) + dot(t_hi, mid))
        y2[pl.ds(s, members, stride=rows), :] = mixed + dot(t_hi, hi)

    def push_out(t, carry):
        peer = (me + t) % n_grid
        send(
            y.at[pl.ds(slot_of(peer) * slab, slab)],
            out.at[:, pl.ds(pl.multiple_of(me * rows, rows), rows), :],
            out_sem, peer, lev,
        )
        return carry

    lax.fori_loop(1, n_grid, push_out, 0)
    out[:, pl.ds(pl.multiple_of(me * rows, rows), rows), :] = y[pl.ds(my_slot * slab, slab)]
    drain(y.at[pl.ds(0, members - slab)], out_sem.at[1])

    drain(gath.at[pl.ds(0, (n_z - 1) * prow), :], z_sem.at[0])
    drain(gath.at[pl.ds(0, (n_y - 1) * n_z * prow), :], y_sem.at[0])
    drain(gath.at[pl.ds(0, half), :], c_sem.at[0])
    drain(f.at[pl.ds(0, members - slab)], in_sem.at[0])
    drain(y.at[pl.ds(0, members - slab)], out_sem.at[0])
    for b in range(NB):
        drain(srecv.at[b], s_sem.at[b, 0])
    for b in range(NB - 1):
        drain(crecv.at[b], r_sem.at[b, 0])


def body(n_grid, n_lev, prior_fields, channel_weights, obs_owner, obs_offset, obs_value, obs_error, ancestors):
    slab, depth, cells = prior_fields.shape
    tiles = cells // LANES
    x = prior_fields.reshape(slab, depth, tiles, LANES).transpose(0, 2, 1, 3).reshape(slab, tiles * depth, LANES)
    members = slab * n_grid
    rows = tiles * depth // n_grid
    count = obs_offset.shape[2]
    vm = pl.BlockSpec(memory_space=pltpu.VMEM)
    sm = pl.BlockSpec(memory_space=pltpu.SMEM)
    pair = pltpu.SemaphoreType.DMA((2,))
    out = pl.pallas_call(
        functools.partial(kernel, n_grid, n_lev),
        out_shape=jax.ShapeDtypeStruct((slab, tiles * depth, LANES), F32),
        in_specs=[sm, sm, vm, vm, vm, vm, vm],
        out_specs=vm,
        scratch_shapes=[
            pltpu.VMEM((24, LANES), F32),
            pltpu.VMEM((24 * n_grid, LANES), F32),
            pltpu.VMEM((members, rows, LANES), F32),
            pltpu.VMEM((members, rows, LANES), F32),
            pltpu.VMEM((len(PAIRS), members, n_lev * count), F32),
            pltpu.VMEM((NB, n_lev, members // 2, LANES), F32),
            pltpu.VMEM((NB, n_lev - 1, members // 2, LANES), F32),
            pltpu.VMEM((NB - 1, n_lev, 8, LANES), F32),
            pltpu.VMEM((NB - 1, n_lev - 1, 8, LANES), F32),
            pair, pair, pair, pair, pair,
            pltpu.SemaphoreType.DMA((NB, 2)),
            pltpu.SemaphoreType.DMA((NB - 1, 2)),
        ],
        compiler_params=pltpu.CompilerParams(has_side_effects=True, vmem_limit_bytes=40 * 1024 * 1024),
    )(obs_owner, channel_weights, x, obs_offset, obs_value, obs_error, ancestors.reshape(NB, 1, members))
    return out.reshape(slab, tiles, depth, LANES).transpose(0, 2, 1, 3).reshape(slab, depth, cells)


def solution(mesh):
    in_specs = (
        P("grid", "lev", None),
        P("lev", None),
        P(),
        P(),
        P(None, "lev", None),
        P(None, "lev", None),
        P(None, "lev", "grid", None),
    )
    out_specs = P("grid", "lev", None)
    step = functools.partial(body, mesh.shape["grid"], mesh.shape["lev"])
    return jax.shard_map(step, mesh=mesh, in_specs=in_specs, out_specs=out_specs, check_vma=False)
```

```python
import functools

import jax
import jax.numpy as jnp
from jax import lax
from jax.experimental import pallas as pl
from jax.experimental.pallas import tpu as pltpu
from jax.sharding import PartitionSpec as P

NB = 4
LANES = 128
F32 = jnp.float32
BF16 = jnp.bfloat16
MESH = pl.DeviceIdType.MESH
BASE_ROW = (0, 8, 12, 16)
PAIRS = [(1, 0), (2, 0), (2, 1), (3, 0), (3, 1), (3, 2)]


def iota(shape, axis):
    return lax.broadcasted_iota(jnp.int32, shape, axis)


def split3(v):
    hi = v.astype(BF16)
    rest = v - hi.astype(F32)
    mid = rest.astype(BF16)
    low = (rest - mid.astype(F32)).astype(BF16)
    return hi, mid, low


def dot(a, b):
    return jnp.dot(a, b, preferred_element_type=F32)


def pick_dot(onehot, v):
    hi, mid, low = split3(v)
    return (dot(onehot, low) + dot(onehot, mid)) + dot(onehot, hi)


def kernel(
    n_grid, n_lev, owner_h, cw_h, x_h, off_h, val_h, err_h, anc_h, out,
    owner, cw, x, off, val, err, anc, pay, zbuf, first, picks, gath, f, y, ys, ssend, srecv, csend, crecv, tiles_s,
    load_sem, z_sem, f_sem, p_sem, g_sem, in_sem, out_sem, s_sem, r_sem,
):
    slab = x.shape[0]
    rows = x.shape[1] // n_grid
    members = slab * n_grid
    half = members // 2
    count = off.shape[2]
    block = rows * LANES // 2
    n_core, n_y = 2, 4
    n_z = n_grid // (n_core * n_y)
    n_col = n_core * n_y
    scale = n_grid / 2.0

    me = lax.axis_index("grid")
    lev = lax.axis_index("lev")
    core = me % n_core
    yy = (me // n_core) % n_y
    zz = me // n_col

    def slot_of(g):
        return (g % n_core) * (n_y * n_z) + ((g // n_core) % n_y) * n_z + g // n_col

    def grid_of(s):
        return ((s % n_z) * n_y + (s // n_z) % n_y) * n_core + s // (n_z * n_y)

    my_slot = slot_of(me)
    my_col = core * n_y + yy

    def col_peer(d):
        return zz * n_col + (me + d) % n_col

    loads = []
    for k, (src, dst) in enumerate(
        [(x_h, x), (owner_h, owner), (off_h, off), (cw_h, cw), (anc_h, anc), (val_h, val), (err_h, err)]
    ):
        copy = pltpu.make_async_copy(src, dst, load_sem.at[k])
        copy.start()
        loads.append(copy)

    barrier = pltpu.get_barrier_semaphore()

    def hello(grid, level):
        pl.semaphore_signal(barrier, inc=1, device_id=(grid, level), device_id_type=MESH)

    for d in range(1, n_z):
        hello((me + d * n_col) % n_grid, lev)
    for e in range(n_lev):
        for d in range(n_col):
            if d or e:
                hello(col_peer(d), (lev + e) % n_lev)

    def send(src, dst, sem, grid, level):
        pltpu.make_async_remote_copy(
            src_ref=src, dst_ref=dst, send_sem=sem.at[0], recv_sem=sem.at[1],
            device_id=(grid, level), device_id_type=MESH,
        ).start()

    def drain(ref, sem):
        pltpu.make_async_copy(ref, ref, sem).wait()

    for copy in loads:
        copy.wait()

    lane256 = iota((1, n_lev * count), 1)
    wrow = []
    for level in range(2):
        w = jnp.zeros((1, n_lev * count), F32)
        for g in range(n_lev):
            w = jnp.where(lane256 // count == g, cw[level, g], w)
        wrow.append(w)
    row16 = iota((slab * rows, n_lev * count), 0)
    weights = jnp.where(row16 % 2 == 0, wrow[0], wrow[1])
    tile_of_row = (row16 % rows) // 2

    def scan_blocks(k, tiles):
        tile = x[:, pl.ds(pl.multiple_of(k * rows, rows), rows), :]
        return tuple(jnp.where(owner[b] == k, tile, kept) for b, kept in enumerate(tiles))

    zero = jnp.zeros((slab, rows, LANES), F32)
    tiles = lax.fori_loop(0, n_grid, scan_blocks, (zero,) * NB, unroll=8)
    pay[...] = jnp.zeros_like(pay)
    for b in range(NB):
        src = tiles[b].reshape(slab * rows, LANES)
        cells = jnp.concatenate([off[b, g : g + 1, :] for g in range(n_lev)], axis=1)
        onehot = (iota((LANES, n_lev * count), 0) == cells % LANES).astype(BF16)
        hi, mid, low = split3(src)
        got = (dot(low, onehot) + dot(mid, onehot)) + dot(hi, onehot)
        got = jnp.where(tile_of_row == cells // LANES, got * weights, 0.0)
        for i in range(slab):
            value = jnp.sum(got[i * rows : (i + 1) * rows], axis=0, keepdims=True)
            for h in range(2):
                at = BASE_ROW[b] + h * 2 + i
                pay[at : at + 1, :] = value[:, h * LANES : (h + 1) * LANES]
        if b < NB - 1:
            pay[4 + b : 5 + b, :] = anc[b].astype(F32)

    pl.semaphore_wait(barrier, n_z - 1 + n_lev * n_col - 1)

    for d in range(1, n_z):
        send(pay, zbuf.at[zz], z_sem, (me + d * n_col) % n_grid, lev)
    zbuf[zz] = pay[...]

    lane1 = iota((1, LANES), 1)
    low8 = iota((n_z, LANES), 1) < count
    member_lane = iota((members, members), 1)
    eye = (iota((members, members), 0) == member_lane).astype(F32)

    taper = {}
    alpha = {}
    for b in range(NB):
        cells = off[b, pl.ds(lev, 1), :]
        where = (owner[b] * block + cells).astype(F32) / block
        where = jnp.concatenate([where, where], axis=1)
        regions = {0: me}
        for later in range(b + 1, NB):
            regions[later] = owner[later]
        for key, region in regions.items():
            distance = ((region.astype(F32) + 0.5) - where) / scale
            t = jnp.exp(-0.5 * distance * distance)
            taper[b, key] = t
            total = jnp.sum(t, axis=1, keepdims=True)
            alpha[b, key] = 0.8 * (1.0 - jnp.exp(-total / (2 * count)))

    drain(zbuf.at[pl.ds(0, n_z - 1)], z_sem.at[1])
    z2 = zbuf.reshape(n_z * 24, LANES)
    for g in range(n_lev):
        a = z2[pl.ds((g // 2) * 2, n_z, stride=24), :]
        c = z2[pl.ds((g // 2) * 2 + 1, n_z, stride=24), :]
        tiles_s[g] = jnp.where(low8, a, pltpu.roll(c, count, 1)) if g % 2 == 0 else jnp.where(low8, pltpu.roll(a, count, 1), c)
    for e in range(n_lev):
        level = (lev + e) % n_lev
        for d in range(n_col):
            if d or e:
                send(tiles_s.at[level], first.at[lev * n_col + my_col], f_sem, col_peer(d), level)
    first[lev * n_col + my_col] = tiles_s[lev]

    z_of_row = iota((n_z, LANES), 0)
    rows_of = [z2[pl.ds(4 + i, n_z, stride=24), :] for i in range(NB - 1)]
    found = [
        jnp.sum(jnp.where(z_of_row * n_col + yy * n_core + core == owner[b], rows_of[i], 0.0), axis=0, keepdims=True)
        for b, i in PAIRS
    ]
    tiles_s[n_lev] = jnp.concatenate(found + found[:2], axis=0)
    for d in range(1, n_col):
        send(tiles_s.at[n_lev], picks.at[my_col], p_sem, col_peer(d), lev)
    picks[my_col] = tiles_s[n_lev]
    for k in range(2):
        mine = zbuf.at[:, pl.ds(8 + 8 * k, 8), :]
        for d in range(1, n_col):
            send(mine, gath.at[k, pl.ds(my_col * n_z, n_z)], g_sem.at[k], col_peer(d), lev)
        gath[k, pl.ds(my_col * n_z, n_z)] = zbuf[:, 8 + 8 * k : 16 + 8 * k, :]

    def push_in(t, carry):
        peer = (me + t) % n_grid
        send(
            x.at[:, pl.ds(pl.multiple_of(peer * rows, rows), rows), :],
            f.at[pl.ds(my_slot * slab, slab)],
            in_sem, peer, lev,
        )
        return carry

    lax.fori_loop(1, n_grid, push_in, 0)
    f[pl.ds(my_slot * slab, slab)] = x[:, pl.ds(pl.multiple_of(me * rows, rows), rows), :]

    sub = iota((members, members), 0)
    perm = (grid_of(sub % n_grid) * slab + sub // n_grid == member_lane).astype(BF16)

    def columns(stack):
        stack = stack.astype(jnp.int32)
        stack = (slot_of(stack // slab) + (stack % slab) * n_grid).astype(F32).astype(BF16)
        return lax.dot_general(perm, stack, (((1,), (1,)), ((), ())), preferred_element_type=F32)

    def picker(cols, k):
        return (cols[:, k : k + 1].astype(jnp.int32) == member_lane).astype(BF16)

    own = [anc[b].astype(F32) for b in range(NB)]
    own_cols = columns(jnp.concatenate(own + own, axis=0))
    chain = [eye]
    for b in range(NB):
        a = alpha[b, 0]
        chosen = picker(own_cols, b)
        moved = chosen.astype(F32) if b == 0 else pick_dot(chosen, chain[b])
        chain.append(a * moved + (1.0 - a) * chain[b])

    low_half = iota((half, LANES), 1) < count
    shift = {b: jnp.zeros((1, n_lev * count), F32) for b in range(1, NB)}
    mean_row = jnp.zeros((1, members), F32)

    def exchange_base(b, v):
        top, bottom = v[:half], v[half:]
        for g in range(n_lev):
            lanes = slice((g // 2) * LANES, (g // 2 + 1) * LANES)
            a, c = top[:, lanes], bottom[:, lanes]
            if g % 2 == 0:
                packed = jnp.where(low_half, a, pltpu.roll(c, count, 1))
            else:
                packed = jnp.where(low_half, pltpu.roll(a, count, 1), c)
            ssend[b - 1, g] = packed
        for d in range(1, n_lev):
            level = (lev + d) % n_lev
            send(ssend.at[b - 1, level], srecv.at[b - 1, d - 1], s_sem.at[b - 1], me, level)

    def base(b, pair_cols):
        k, r = (b - 1) // 2, ((b - 1) % 2) * 4
        g2 = gath.reshape(2 * n_grid * 8, LANES)
        parts = []
        for h in range(2):
            two = [g2[pl.ds(k * n_grid * 8 + r + h * 2 + i, n_grid, stride=8), :] for i in range(slab)]
            parts.append(jnp.concatenate(two, axis=0))
        v = jnp.concatenate(parts, axis=1)
        for i in range(b):
            ys[PAIRS.index((b, i))] = v
            a = alpha[i, b]
            v = a * pick_dot(picker(pair_cols, PAIRS.index((b, i))), v) + (1.0 - a) * v
        exchange_base(b, v)

    def weigh(b, prior):
        row = jnp.zeros((1, members), F32)
        seen = jnp.concatenate([val[b], val[b]], axis=1)
        dev = jnp.concatenate([err[b], err[b]], axis=1)
        innovation = ((seen - prior) / dev) ** 2
        for key in list(range(b + 1, NB)) + [0]:
            weighted = innovation * taper[b, key]
            top = jnp.sum(jnp.where(low_half, weighted, 0.0), axis=1, keepdims=True)
            bottom = jnp.sum(jnp.where(low_half, 0.0, weighted), axis=1, keepdims=True)
            log_weight = (-0.5 / count) * jnp.concatenate([top, bottom], axis=0)
            expo = jnp.exp(log_weight - jnp.max(log_weight, axis=0, keepdims=True))
            change = expo / jnp.sum(expo, axis=0, keepdims=True) - 1.0 / members
            if key == 0:
                row = jnp.sum(change * chain[b], axis=0, keepdims=True)
            else:
                shift[key] = shift[key] + jnp.sum(change * ys[PAIRS.index((key, b))], axis=0, keepdims=True)
                if key == b + 1:
                    push_shift(key)
        return row

    def push_shift(b):
        for g in range(n_lev):
            row = shift[b][:, (g // 2) * LANES : (g // 2 + 1) * LANES]
            other = pltpu.roll(row, count, 1)
            left = lane1 < count
            row = jnp.where(left, row, other) if g % 2 == 0 else jnp.where(left, other, row)
            csend[b - 1, g] = jnp.broadcast_to(row, (8, LANES))
        for d in range(1, n_lev):
            level = (lev + d) % n_lev
            send(csend.at[b - 1, level], crecv.at[b - 1, d - 1], r_sem.at[b - 1], me, level)

    drain(picks.at[pl.ds(0, n_col - 1)], p_sem.at[1])
    chosen = picks[0]
    for k in range(1, n_col):
        chosen = chosen + picks[k]
    pair_cols = columns(chosen)
    drain(gath.at[0, pl.ds(0, (n_col - 1) * n_z)], g_sem.at[0, 1])
    base(1, pair_cols)
    base(2, pair_cols)
    drain(gath.at[1, pl.ds(0, (n_col - 1) * n_z)], g_sem.at[1, 1])
    base(3, pair_cols)

    drain(first.at[pl.ds(0, n_lev * n_col - 1)], f_sem.at[1])
    prior = first[:n_col]
    for level in range(1, n_lev):
        prior = prior + first[level * n_col : (level + 1) * n_col]
    mean_row = weigh(0, prior.reshape(half, LANES))
    for b in range(1, NB):
        drain(srecv.at[b - 1], s_sem.at[b - 1, 1])
        prior = ssend[b - 1, lev]
        for d in range(n_lev - 1):
            prior = prior + srecv[b - 1, d]
        drain(crecv.at[b - 1], r_sem.at[b - 1, 1])
        row = csend[b - 1, lev]
        for d in range(n_lev - 1):
            row = row + crecv[b - 1, d]
        mean_row = mean_row + weigh(b, prior + row[0:1, :])

    total = chain[NB] + mean_row
    t_hi, t_mid, t_low = split3(total)
    drain(f.at[pl.ds(0, members - slab)], in_sem.at[1])
    f2 = f.reshape(members * rows, LANES)
    y2 = y.reshape(members * rows, LANES)
    for s in range(rows):
        two = [f2[pl.ds(i * rows + s, n_grid, stride=slab * rows), :] for i in range(slab)]
        hi, mid, low = split3(jnp.concatenate(two, axis=0))
        mixed = (dot(t_low, hi) + dot(t_mid, mid)) + dot(t_hi, low)
        mixed = mixed + (dot(t_mid, hi) + dot(t_hi, mid))
        mixed = mixed + dot(t_hi, hi)
        for i in range(slab):
            y2[pl.ds(i * rows + s, n_grid, stride=slab * rows), :] = mixed[i * n_grid : (i + 1) * n_grid]

    def push_out(t, carry):
        peer = (me + t) % n_grid
        send(
            y.at[pl.ds(slot_of(peer) * slab, slab)],
            out.at[:, pl.ds(pl.multiple_of(me * rows, rows), rows), :],
            out_sem, peer, lev,
        )
        return carry

    lax.fori_loop(1, n_grid, push_out, 0)
    keep = pltpu.make_async_copy(
        y.at[pl.ds(my_slot * slab, slab)], out.at[:, pl.ds(pl.multiple_of(me * rows, rows), rows), :], load_sem.at[0]
    )
    keep.start()
    keep.wait()

    drain(zbuf.at[pl.ds(0, n_z - 1)], z_sem.at[0])
    drain(first.at[pl.ds(0, n_lev * n_col - 1)], f_sem.at[0])
    drain(picks.at[pl.ds(0, n_col - 1)], p_sem.at[0])
    for k in range(2):
        drain(gath.at[0, pl.ds(0, (n_col - 1) * n_z)], g_sem.at[k, 0])
    drain(f.at[pl.ds(0, members - slab)], in_sem.at[0])
    for b in range(NB - 1):
        drain(srecv.at[b], s_sem.at[b, 0])
        drain(crecv.at[b], r_sem.at[b, 0])
    drain(y.at[pl.ds(0, members - slab)], out_sem.at[1])
    drain(y.at[pl.ds(0, members - slab)], out_sem.at[0])


def body(n_grid, n_lev, prior_fields, channel_weights, obs_owner, obs_offset, obs_value, obs_error, ancestors):
    slab, depth, cells = prior_fields.shape
    tiles = cells // LANES
    x = prior_fields.reshape(slab, depth, tiles, LANES).transpose(0, 2, 1, 3).reshape(slab, tiles * depth, LANES)
    members = slab * n_grid
    rows = tiles * depth // n_grid
    count = obs_offset.shape[2]
    n_col = 8
    n_z = n_grid // n_col
    vm = pl.BlockSpec(memory_space=pltpu.VMEM)
    hbm = pl.BlockSpec(memory_space=pltpu.HBM)
    pair = pltpu.SemaphoreType.DMA((2,))
    out = pl.pallas_call(
        functools.partial(kernel, n_grid, n_lev),
        out_shape=jax.ShapeDtypeStruct((slab, tiles * depth, LANES), F32),
        in_specs=[hbm] * 7,
        out_specs=hbm,
        scratch_shapes=[
            pltpu.SMEM(obs_owner.shape, jnp.int32),
            pltpu.SMEM(channel_weights.shape, F32),
            pltpu.VMEM(x.shape, F32),
            pltpu.VMEM(obs_offset.shape, jnp.int32),
            pltpu.VMEM(obs_value.shape, F32),
            pltpu.VMEM(obs_error.shape, F32),
            pltpu.VMEM((NB, 1, members), jnp.int32),
            pltpu.VMEM((24, LANES), F32),
            pltpu.VMEM((n_z, 24, LANES), F32),
            pltpu.VMEM((n_lev * n_col, n_z, LANES), F32),
            pltpu.VMEM((n_col, 8, LANES), F32),
            pltpu.VMEM((2, n_grid, 8, LANES), F32),
            pltpu.VMEM((members, rows, LANES), F32),
            pltpu.VMEM((members, rows, LANES), F32),
            pltpu.VMEM((len(PAIRS), members, n_lev * count), F32),
            pltpu.VMEM((NB - 1, n_lev, members // 2, LANES), F32),
            pltpu.VMEM((NB - 1, n_lev - 1, members // 2, LANES), F32),
            pltpu.VMEM((NB - 1, n_lev, 8, LANES), F32),
            pltpu.VMEM((NB - 1, n_lev - 1, 8, LANES), F32),
            pltpu.VMEM((n_lev + 1, 8, LANES), F32),
            pltpu.SemaphoreType.DMA((7,)),
            pair, pair, pair,
            pltpu.SemaphoreType.DMA((2, 2)),
            pair, pair,
            pltpu.SemaphoreType.DMA((NB - 1, 2)),
            pltpu.SemaphoreType.DMA((NB - 1, 2)),
        ],
        compiler_params=pltpu.CompilerParams(
            has_side_effects=True, collective_id=0, vmem_limit_bytes=56 * 1024 * 1024
        ),
    )(obs_owner, channel_weights, x, obs_offset, obs_value, obs_error, ancestors.reshape(NB, 1, members))
    return out.reshape(slab, tiles, depth, LANES).transpose(0, 2, 1, 3).reshape(slab, depth, cells)


def solution(mesh):
    in_specs = (
        P("grid", "lev", None),
        P("lev", None),
        P(),
        P(),
        P(None, "lev", None),
        P(None, "lev", None),
        P(None, "lev", "grid", None),
    )
    out_specs = P("grid", "lev", None)
    step = functools.partial(body, mesh.shape["grid"], mesh.shape["lev"])
    return jax.shard_map(step, mesh=mesh, in_specs=in_specs, out_specs=out_specs, check_vma=False)
```

```python
import functools

import jax
import jax.numpy as jnp
from jax import lax
from jax.experimental import pallas as pl
from jax.experimental.pallas import tpu as pltpu
from jax.sharding import PartitionSpec as P

NB = 4
LANES = 128
F32 = jnp.float32
BF16 = jnp.bfloat16
MESH = pl.DeviceIdType.MESH
BASE_ROW = (0, 8, 12, 16)
BATCH_TILE = 5
CUTS = (1, 64, 64, 64, 64, 64, 64, 64)
PAIRS = [(1, 0), (2, 0), (2, 1), (3, 0), (3, 1), (3, 2)]


def iota(shape, axis):
    return lax.broadcasted_iota(jnp.int32, shape, axis)


def split3(v):
    hi = v.astype(BF16)
    rest = v - hi.astype(F32)
    mid = rest.astype(BF16)
    low = (rest - mid.astype(F32)).astype(BF16)
    return hi, mid, low


def dot(a, b):
    return jnp.dot(a, b, preferred_element_type=F32)


def pick_dot(onehot, v):
    hi, mid, low = split3(v)
    return (dot(onehot, low) + dot(onehot, mid)) + dot(onehot, hi)


def kernel(
    n_grid, n_lev, owner_h, cw_h, x_h, off_h, val_h, err_h, anc_h, out,
    owner, cw, x, off, val, err, anc, pay, zbuf, first, picks, gath, f, y, ys, ssend, srecv, csend, crecv, tiles_s,
    load_sem, z_sem, f_sem, p_sem, g_sem, in_sem, out_sem, s_sem, r_sem,
):
    slab = x.shape[0]
    rows = x.shape[1] // n_grid
    members = slab * n_grid
    half = members // 2
    count = off.shape[2]
    block = rows * LANES // 2
    n_core, n_y = 2, 4
    n_z = n_grid // (n_core * n_y)
    n_col = n_core * n_y
    scale = n_grid / 2.0

    me = lax.axis_index("grid")
    lev = lax.axis_index("lev")
    core = me % n_core
    yy = (me // n_core) % n_y
    zz = me // n_col

    def slot_of(g):
        return (g % n_core) * (n_y * n_z) + ((g // n_core) % n_y) * n_z + g // n_col

    def grid_of(s):
        return ((s % n_z) * n_y + (s // n_z) % n_y) * n_core + s // (n_z * n_y)

    my_slot = slot_of(me)
    my_col = core * n_y + yy

    def col_peer(d):
        return zz * n_col + (me + d) % n_col

    loads = []
    for k, (src, dst) in enumerate(
        [(x_h, x), (owner_h, owner), (off_h, off), (cw_h, cw), (anc_h, anc), (val_h, val), (err_h, err)]
    ):
        copy = pltpu.make_async_copy(src, dst, load_sem.at[k])
        copy.start()
        loads.append(copy)

    barrier = pltpu.get_barrier_semaphore()

    def hello(grid, level):
        pl.semaphore_signal(barrier, inc=1, device_id=(grid, level), device_id_type=MESH)

    for d in range(1, n_z):
        hello((me + d * n_col) % n_grid, lev)
    for e in range(n_lev):
        for d in range(n_col):
            if d or e:
                hello(col_peer(d), (lev + e) % n_lev)

    def send(src, dst, sem, grid, level):
        pltpu.make_async_remote_copy(
            src_ref=src, dst_ref=dst, send_sem=sem.at[0], recv_sem=sem.at[1],
            device_id=(grid, level), device_id_type=MESH,
        ).start()

    def drain(ref, sem):
        pltpu.make_async_copy(ref, ref, sem).wait()

    for copy in loads:
        copy.wait()

    lane256 = iota((1, n_lev * count), 1)
    wrow = []
    for level in range(2):
        w = jnp.zeros((1, n_lev * count), F32)
        for g in range(n_lev):
            w = jnp.where(lane256 // count == g, cw[level, g], w)
        wrow.append(w)
    row16 = iota((slab * rows, n_lev * count), 0)
    weights = jnp.where(row16 % 2 == 0, wrow[0], wrow[1])
    tile_of_row = (row16 % rows) // 2

    def scan_blocks(k, tiles):
        tile = x[:, pl.ds(pl.multiple_of(k * rows, rows), rows), :]
        return tuple(jnp.where(owner[b] == k, tile, kept) for b, kept in enumerate(tiles))

    zero = jnp.zeros((slab, rows, LANES), F32)
    tiles = lax.fori_loop(0, n_grid, scan_blocks, (zero,) * NB, unroll=8)
    pay[...] = jnp.zeros_like(pay)
    for b in range(NB):
        src = tiles[b].reshape(slab * rows, LANES)
        cells = jnp.concatenate([off[b, g : g + 1, :] for g in range(n_lev)], axis=1)
        onehot = (iota((LANES, n_lev * count), 0) == cells % LANES).astype(BF16)
        hi, mid, low = split3(src)
        got = (dot(low, onehot) + dot(mid, onehot)) + dot(hi, onehot)
        got = jnp.where(tile_of_row == cells // LANES, got * weights, 0.0)
        for i in range(slab):
            value = jnp.sum(got[i * rows : (i + 1) * rows], axis=0, keepdims=True)
            for h in range(2):
                at = BASE_ROW[b] + h * 2 + i
                pay[at : at + 1, :] = value[:, h * LANES : (h + 1) * LANES]
        if b < NB - 1:
            pay[4 + b : 5 + b, :] = anc[b].astype(F32)

    pl.semaphore_wait(barrier, n_z - 1 + n_lev * n_col - 1)

    for d in range(1, n_z):
        send(pay, zbuf.at[zz], z_sem, (me + d * n_col) % n_grid, lev)
    zbuf[zz] = pay[...]

    lane1 = iota((1, LANES), 1)
    low8 = iota((n_z, LANES), 1) < count
    member_lane = iota((members, members), 1)
    eye = (iota((members, members), 0) == member_lane).astype(F32)

    taper = {}
    alpha = {}
    for b in range(NB):
        cells = off[b, pl.ds(lev, 1), :]
        where = (owner[b] * block + cells).astype(F32) / block
        where = jnp.concatenate([where, where], axis=1)
        regions = {0: me}
        for later in range(b + 1, NB):
            regions[later] = owner[later]
        for key, region in regions.items():
            distance = ((region.astype(F32) + 0.5) - where) / scale
            t = jnp.exp(-0.5 * distance * distance)
            taper[b, key] = t
            total = jnp.sum(t, axis=1, keepdims=True)
            alpha[b, key] = 0.8 * (1.0 - jnp.exp(-total / (2 * count)))

    sub = iota((members, members), 0)
    perm = (grid_of(sub % n_grid) * slab + sub // n_grid == member_lane).astype(BF16)

    def columns(stack):
        stack = stack.astype(jnp.int32)
        stack = (slot_of(stack // slab) + (stack % slab) * n_grid).astype(F32).astype(BF16)
        return lax.dot_general(perm, stack, (((1,), (1,)), ((), ())), preferred_element_type=F32)

    def picker(cols, k):
        return (cols[:, k : k + 1].astype(jnp.int32) == member_lane).astype(BF16)

    own = [anc[b].astype(F32) for b in range(NB)]
    own_cols = columns(jnp.concatenate(own + own, axis=0))
    chain = [eye]
    for b in range(NB):
        a = alpha[b, 0]
        chosen = picker(own_cols, b)
        moved = chosen.astype(F32) if b == 0 else pick_dot(chosen, chain[b])
        chain.append(a * moved + (1.0 - a) * chain[b])

    drain(zbuf.at[pl.ds(0, n_z - 1)], z_sem.at[1])
    z2 = zbuf.reshape(n_z * 24, LANES)
    for g in range(n_lev):
        a = z2[pl.ds((g // 2) * 2, n_z, stride=24), :]
        c = z2[pl.ds((g // 2) * 2 + 1, n_z, stride=24), :]
        tiles_s[g] = jnp.where(low8, a, pltpu.roll(c, count, 1)) if g % 2 == 0 else jnp.where(low8, pltpu.roll(a, count, 1), c)
    for e in range(n_lev):
        level = (lev + e) % n_lev
        for d in range(n_col):
            if d or e:
                send(tiles_s.at[level], first.at[lev * n_col + my_col], f_sem, col_peer(d), level)
    first[lev * n_col + my_col] = tiles_s[lev]

    z_of_row = iota((n_z, LANES), 0)
    rows_of = [z2[pl.ds(4 + i, n_z, stride=24), :] for i in range(NB - 1)]
    found = [
        jnp.sum(jnp.where(z_of_row * n_col + yy * n_core + core == owner[b], rows_of[i], 0.0), axis=0, keepdims=True)
        for b, i in PAIRS
    ]
    tiles_s[n_lev] = jnp.concatenate(found + found[:2], axis=0)
    for d in range(1, n_col):
        send(tiles_s.at[n_lev], picks.at[my_col], p_sem, col_peer(d), lev)
    picks[my_col] = tiles_s[n_lev]
    for b in range(1, NB):
        for r in range(4):
            tiles_s[BATCH_TILE + 4 * (b - 1) + r] = z2[pl.ds(BASE_ROW[b] + r, n_z, stride=24), :]
        mine = tiles_s.at[pl.ds(BATCH_TILE + 4 * (b - 1), 4)]
        for d in range(1, n_col):
            send(mine, gath.at[b - 1, my_col], g_sem.at[b - 1], col_peer(d), lev)
        gath[b - 1, my_col] = tiles_s[BATCH_TILE + 4 * (b - 1) : BATCH_TILE + 4 * b]

    def push_in(t, carry):
        far = (t + 1) // 2
        peer = (me + far + (1 - t % 2) * (n_grid - 2 * far)) % n_grid
        send(
            x.at[:, pl.ds(pl.multiple_of(peer * rows, rows), rows), :],
            f.at[pl.ds(my_slot * slab, slab)],
            in_sem, peer, lev,
        )
        return carry

    def push_blocks(k):
        lax.fori_loop(CUTS[k], CUTS[k + 1], push_in, 0)

    push_blocks(0)
    f[pl.ds(my_slot * slab, slab)] = x[:, pl.ds(pl.multiple_of(me * rows, rows), rows), :]

    low_half = iota((half, LANES), 1) < count
    shift = {b: jnp.zeros((1, n_lev * count), F32) for b in range(1, NB)}

    def exchange_base(b, v):
        top, bottom = v[:half], v[half:]
        for g in range(n_lev):
            lanes = slice((g // 2) * LANES, (g // 2 + 1) * LANES)
            a, c = top[:, lanes], bottom[:, lanes]
            if g % 2 == 0:
                packed = jnp.where(low_half, a, pltpu.roll(c, count, 1))
            else:
                packed = jnp.where(low_half, pltpu.roll(a, count, 1), c)
            ssend[b - 1, g] = packed
        for d in range(1, n_lev):
            level = (lev + d) % n_lev
            send(ssend.at[b - 1, level], srecv.at[b - 1, d - 1], s_sem.at[b - 1], me, level)

    def member_values(b):
        parts = []
        for h in range(2):
            two = [gath[b - 1, :, h * 2 + i].reshape(n_grid, LANES) for i in range(slab)]
            parts.append(jnp.concatenate(two, axis=0))
        return jnp.concatenate(parts, axis=1)

    def base(b, v, pair_cols):
        for i in range(b):
            ys[PAIRS.index((b, i))] = v
            a = alpha[i, b]
            v = a * pick_dot(picker(pair_cols, PAIRS.index((b, i))), v) + (1.0 - a) * v
        exchange_base(b, v)

    def weigh(b, prior):
        seen = jnp.concatenate([val[b], val[b]], axis=1)
        dev = jnp.concatenate([err[b], err[b]], axis=1)
        innovation = ((seen - prior) / dev) ** 2
        changes = {}
        for key in list(range(b + 1, NB)) + [0]:
            weighted = innovation * taper[b, key]
            top = jnp.sum(jnp.where(low_half, weighted, 0.0), axis=1, keepdims=True)
            bottom = jnp.sum(jnp.where(low_half, 0.0, weighted), axis=1, keepdims=True)
            log_weight = (-0.5 / count) * jnp.concatenate([top, bottom], axis=0)
            expo = jnp.exp(log_weight - jnp.max(log_weight, axis=0, keepdims=True))
            changes[key] = expo / jnp.sum(expo, axis=0, keepdims=True) - 1.0 / members
        return changes

    def move(b, change, v):
        shift[b] = shift[b] + jnp.sum(change * v, axis=0, keepdims=True)

    def push_shift(b):
        for g in range(n_lev):
            row = shift[b][:, (g // 2) * LANES : (g // 2 + 1) * LANES]
            other = pltpu.roll(row, count, 1)
            left = lane1 < count
            row = jnp.where(left, row, other) if g % 2 == 0 else jnp.where(left, other, row)
            csend[b - 1, g] = jnp.broadcast_to(row, (8, LANES))
        for d in range(1, n_lev):
            level = (lev + d) % n_lev
            send(csend.at[b - 1, level], crecv.at[b - 1, d - 1], r_sem.at[b - 1], me, level)

    def full_prior(b):
        drain(srecv.at[b - 1], s_sem.at[b - 1, 1])
        prior = ssend[b - 1, lev]
        for d in range(n_lev - 1):
            prior = prior + srecv[b - 1, d]
        drain(crecv.at[b - 1], r_sem.at[b - 1, 1])
        row = csend[b - 1, lev]
        for d in range(n_lev - 1):
            row = row + crecv[b - 1, d]
        return prior + row[0:1, :]

    drain(first.at[pl.ds(0, n_lev * n_col - 1)], f_sem.at[1])
    prior = first[:n_col]
    for level in range(1, n_lev):
        prior = prior + first[level * n_col : (level + 1) * n_col]
    change = {0: weigh(0, prior.reshape(half, LANES))}
    push_blocks(1)

    drain(picks.at[pl.ds(0, n_col - 1)], p_sem.at[1])
    chosen = picks[0]
    for k in range(1, n_col):
        chosen = chosen + picks[k]
    pair_cols = columns(chosen)
    for b in range(1, NB):
        drain(gath.at[b - 1, pl.ds(0, n_col - 1)], g_sem.at[b - 1, 1])
        v = member_values(b)
        if b == 1:
            move(1, change[0][1], v)
            base(1, v, pair_cols)
            push_shift(1)
            push_blocks(2)
        else:
            base(b, v, pair_cols)
            move(b, change[0][b], v)
    push_blocks(3)
    for b in range(1, NB):
        change[b] = weigh(b, full_prior(b))
        for later in range(b + 1, NB):
            move(later, change[b][later], ys[PAIRS.index((later, b))])
            if later == b + 1:
                push_shift(later)
        push_blocks(3 + b)
    mean_row = jnp.zeros((1, members), F32)
    for b in range(NB):
        mean_row = mean_row + jnp.sum(change[b][0] * chain[b], axis=0, keepdims=True)

    total = chain[NB] + mean_row
    t_hi, t_mid, t_low = split3(total)
    drain(f.at[pl.ds(0, members - slab)], in_sem.at[1])
    f2 = f.reshape(members * rows, LANES)
    y2 = y.reshape(members * rows, LANES)
    for s in range(rows):
        two = [f2[pl.ds(i * rows + s, n_grid, stride=slab * rows), :] for i in range(slab)]
        hi, mid, low = split3(jnp.concatenate(two, axis=0))
        mixed = (dot(t_low, hi) + dot(t_mid, mid)) + dot(t_hi, low)
        mixed = mixed + (dot(t_mid, hi) + dot(t_hi, mid))
        mixed = mixed + dot(t_hi, hi)
        for i in range(slab):
            y2[pl.ds(i * rows + s, n_grid, stride=slab * rows), :] = mixed[i * n_grid : (i + 1) * n_grid]

    def push_out(t, carry):
        peer = (me + t) % n_grid
        send(
            y.at[pl.ds(slot_of(peer) * slab, slab)],
            out.at[:, pl.ds(pl.multiple_of(me * rows, rows), rows), :],
            out_sem, peer, lev,
        )
        return carry

    lax.fori_loop(1, n_grid, push_out, 0)
    out[:, pl.ds(pl.multiple_of(me * rows, rows), rows), :] = y[pl.ds(my_slot * slab, slab)]

    drain(zbuf.at[pl.ds(0, n_z - 1)], z_sem.at[0])
    drain(first.at[pl.ds(0, n_lev * n_col - 1)], f_sem.at[0])
    drain(picks.at[pl.ds(0, n_col - 1)], p_sem.at[0])
    for b in range(NB - 1):
        drain(gath.at[b, pl.ds(0, n_col - 1)], g_sem.at[b, 0])
    drain(f.at[pl.ds(0, members - slab)], in_sem.at[0])
    for b in range(NB - 1):
        drain(srecv.at[b], s_sem.at[b, 0])
        drain(crecv.at[b], r_sem.at[b, 0])
    drain(y.at[pl.ds(0, members - slab)], out_sem.at[1])
    drain(y.at[pl.ds(0, members - slab)], out_sem.at[0])


def body(n_grid, n_lev, prior_fields, channel_weights, obs_owner, obs_offset, obs_value, obs_error, ancestors):
    slab, depth, cells = prior_fields.shape
    tiles = cells // LANES
    x = prior_fields.reshape(slab, depth, tiles, LANES).transpose(0, 2, 1, 3).reshape(slab, tiles * depth, LANES)
    members = slab * n_grid
    rows = tiles * depth // n_grid
    count = obs_offset.shape[2]
    n_col = 8
    n_z = n_grid // n_col
    vm = pl.BlockSpec(memory_space=pltpu.VMEM)
    hbm = pl.BlockSpec(memory_space=pltpu.HBM)
    pair = pltpu.SemaphoreType.DMA((2,))
    arrays = (obs_owner, channel_weights, x, obs_offset, obs_value, obs_error, ancestors.reshape(NB, 1, members))
    out = pl.pallas_call(
        functools.partial(kernel, n_grid, n_lev),
        out_shape=jax.ShapeDtypeStruct((slab, tiles * depth, LANES), F32),
        in_specs=[hbm] * 7,
        out_specs=vm,
        scratch_shapes=[
            pltpu.SMEM(obs_owner.shape, jnp.int32),
            pltpu.SMEM(channel_weights.shape, F32),
            pltpu.VMEM(x.shape, F32),
            pltpu.VMEM(obs_offset.shape, jnp.int32),
            pltpu.VMEM(obs_value.shape, F32),
            pltpu.VMEM(obs_error.shape, F32),
            pltpu.VMEM((NB, 1, members), jnp.int32),
            pltpu.VMEM((24, LANES), F32),
            pltpu.VMEM((n_z, 24, LANES), F32),
            pltpu.VMEM((n_lev * n_col, n_z, LANES), F32),
            pltpu.VMEM((n_col, 8, LANES), F32),
            pltpu.VMEM((NB - 1, n_col, 4, n_z, LANES), F32),
            pltpu.VMEM((members, rows, LANES), F32),
            pltpu.VMEM((members, rows, LANES), F32),
            pltpu.VMEM((len(PAIRS), members, n_lev * count), F32),
            pltpu.VMEM((NB - 1, n_lev, members // 2, LANES), F32),
            pltpu.VMEM((NB - 1, n_lev - 1, members // 2, LANES), F32),
            pltpu.VMEM((NB - 1, n_lev, 8, LANES), F32),
            pltpu.VMEM((NB - 1, n_lev - 1, 8, LANES), F32),
            pltpu.VMEM((BATCH_TILE + 4 * (NB - 1), 8, LANES), F32),
            pltpu.SemaphoreType.DMA((7,)),
            pair, pair, pair,
            pltpu.SemaphoreType.DMA((NB - 1, 2)),
            pair, pair,
            pltpu.SemaphoreType.DMA((NB - 1, 2)),
            pltpu.SemaphoreType.DMA((NB - 1, 2)),
        ],
        compiler_params=pltpu.CompilerParams(
            has_side_effects=True, collective_id=0, vmem_limit_bytes=24 * 1024 * 1024
        ),
    )(*[pltpu.with_memory_space_constraint(v, pltpu.HBM) for v in arrays])
    return out.reshape(slab, tiles, depth, LANES).transpose(0, 2, 1, 3).reshape(slab, depth, cells)


def solution(mesh):
    in_specs = (
        P("grid", "lev", None),
        P("lev", None),
        P(),
        P(),
        P(None, "lev", None),
        P(None, "lev", None),
        P(None, "lev", "grid", None),
    )
    out_specs = P("grid", "lev", None)
    step = functools.partial(body, mesh.shape["grid"], mesh.shape["lev"])
    return jax.shard_map(step, mesh=mesh, in_specs=in_specs, out_specs=out_specs, check_vma=False)
```

```python
import functools

import jax
import jax.numpy as jnp
from jax import lax
from jax.experimental import pallas as pl
from jax.experimental.pallas import tpu as pltpu
from jax.sharding import PartitionSpec as P

NB = 4
LANES = 128
F32 = jnp.float32
BF16 = jnp.bfloat16
MESH = pl.DeviceIdType.MESH
BASE_ROW = (0, 8, 12, 16)
BATCH_TILE = 5
CUTS = (1, 64, 64, 64, 64, 64, 64, 64)
PAIRS = [(1, 0), (2, 0), (2, 1), (3, 0), (3, 1), (3, 2)]


def iota(shape, axis):
    return lax.broadcasted_iota(jnp.int32, shape, axis)


def split3(v):
    hi = v.astype(BF16)
    rest = v - hi.astype(F32)
    mid = rest.astype(BF16)
    low = (rest - mid.astype(F32)).astype(BF16)
    return hi, mid, low


def dot(a, b):
    return jnp.dot(a, b, preferred_element_type=F32)


def pick_dot(onehot, v):
    hi, mid, low = split3(v)
    return (dot(onehot, low) + dot(onehot, mid)) + dot(onehot, hi)


def kernel(
    n_grid, n_lev, owner_h, cw_h, x_h, off_h, val_h, err_h, anc_h, out,
    owner, cw, x, off, val, err, anc, pay, zbuf, first, picks, gath, f, y, ys, ssend, srecv, csend, crecv, tiles_s,
    load_sem, z_sem, f_sem, p_sem, y_sem, g_sem, in_sem, out_sem, s_sem, r_sem,
):
    slab = x.shape[0]
    rows = x.shape[1] // n_grid
    members = slab * n_grid
    half = members // 2
    count = off.shape[2]
    block = rows * LANES // 2
    n_core, n_y = 2, 4
    n_z = n_grid // (n_core * n_y)
    n_col = n_core * n_y
    scale = n_grid / 2.0

    me = lax.axis_index("grid")
    lev = lax.axis_index("lev")
    core = me % n_core
    yy = (me // n_core) % n_y
    zz = me // n_col

    def slot_of(g):
        return (g % n_core) * (n_y * n_z) + ((g // n_core) % n_y) * n_z + g // n_col

    def grid_of(s):
        return ((s % n_z) * n_y + (s // n_z) % n_y) * n_core + s // (n_z * n_y)

    my_slot = slot_of(me)
    my_col = core * n_y + yy

    def col_peer(d):
        return zz * n_col + (me + d) % n_col

    loads = []
    for k, (src, dst) in enumerate(
        [(x_h, x), (owner_h, owner), (off_h, off), (cw_h, cw), (anc_h, anc), (val_h, val), (err_h, err)]
    ):
        copy = pltpu.make_async_copy(src, dst, load_sem.at[k])
        copy.start()
        loads.append(copy)

    barrier = pltpu.get_barrier_semaphore()

    def hello(grid, level):
        pl.semaphore_signal(barrier, inc=1, device_id=(grid, level), device_id_type=MESH)

    for d in range(1, n_z):
        hello((me + d * n_col) % n_grid, lev)
    for e in range(n_lev):
        for d in range(n_col):
            if d or e:
                hello(col_peer(d), (lev + e) % n_lev)

    def send(src, dst, sem, grid, level):
        pltpu.make_async_remote_copy(
            src_ref=src, dst_ref=dst, send_sem=sem.at[0], recv_sem=sem.at[1],
            device_id=(grid, level), device_id_type=MESH,
        ).start()

    def drain(ref, sem):
        pltpu.make_async_copy(ref, ref, sem).wait()

    for copy in loads:
        copy.wait()

    lane256 = iota((1, n_lev * count), 1)
    wrow = []
    for level in range(2):
        w = jnp.zeros((1, n_lev * count), F32)
        for g in range(n_lev):
            w = jnp.where(lane256 // count == g, cw[level, g], w)
        wrow.append(w)
    row16 = iota((slab * rows, n_lev * count), 0)
    weights = jnp.where(row16 % 2 == 0, wrow[0], wrow[1])
    tile_of_row = (row16 % rows) // 2

    def scan_blocks(k, tiles):
        tile = x[:, pl.ds(pl.multiple_of(k * rows, rows), rows), :]
        return tuple(jnp.where(owner[b] == k, tile, kept) for b, kept in enumerate(tiles))

    zero = jnp.zeros((slab, rows, LANES), F32)
    tiles = lax.fori_loop(0, n_grid, scan_blocks, (zero,) * NB, unroll=8)
    pay[...] = jnp.zeros_like(pay)
    for b in range(NB):
        src = tiles[b].reshape(slab * rows, LANES)
        cells = jnp.concatenate([off[b, g : g + 1, :] for g in range(n_lev)], axis=1)
        onehot = (iota((LANES, n_lev * count), 0) == cells % LANES).astype(BF16)
        hi, mid, low = split3(src)
        got = (dot(low, onehot) + dot(mid, onehot)) + dot(hi, onehot)
        got = jnp.where(tile_of_row == cells // LANES, got * weights, 0.0)
        for i in range(slab):
            value = jnp.sum(got[i * rows : (i + 1) * rows], axis=0, keepdims=True)
            for h in range(2):
                at = BASE_ROW[b] + h * 2 + i
                pay[at : at + 1, :] = value[:, h * LANES : (h + 1) * LANES]
        if b < NB - 1:
            pay[4 + b : 5 + b, :] = anc[b].astype(F32)

    pl.semaphore_wait(barrier, n_z - 1 + n_lev * n_col - 1)

    for d in range(1, n_z):
        send(pay, zbuf.at[zz], z_sem, (me + d * n_col) % n_grid, lev)
    zbuf[zz] = pay[...]

    lane1 = iota((1, LANES), 1)
    low8 = iota((n_z, LANES), 1) < count
    member_lane = iota((members, members), 1)
    eye = (iota((members, members), 0) == member_lane).astype(F32)

    taper = {}
    alpha = {}
    for b in range(NB):
        cells = off[b, pl.ds(lev, 1), :]
        where = (owner[b] * block + cells).astype(F32) / block
        where = jnp.concatenate([where, where], axis=1)
        regions = {0: me}
        for later in range(b + 1, NB):
            regions[later] = owner[later]
        for key, region in regions.items():
            distance = ((region.astype(F32) + 0.5) - where) / scale
            t = jnp.exp(-0.5 * distance * distance)
            taper[b, key] = t
            total = jnp.sum(t, axis=1, keepdims=True)
            alpha[b, key] = 0.8 * (1.0 - jnp.exp(-total / (2 * count)))

    sub = iota((members, members), 0)
    perm = (grid_of(sub % n_grid) * slab + sub // n_grid == member_lane).astype(BF16)

    def columns(stack):
        stack = stack.astype(jnp.int32)
        stack = (slot_of(stack // slab) + (stack % slab) * n_grid).astype(F32).astype(BF16)
        return lax.dot_general(perm, stack, (((1,), (1,)), ((), ())), preferred_element_type=F32)

    def picker(cols, k):
        return (cols[:, k : k + 1].astype(jnp.int32) == member_lane).astype(BF16)

    own = [anc[b].astype(F32) for b in range(NB)]
    own_cols = columns(jnp.concatenate(own + own, axis=0))
    chain = [eye]
    for b in range(NB):
        a = alpha[b, 0]
        chosen = picker(own_cols, b)
        moved = chosen.astype(F32) if b == 0 else pick_dot(chosen, chain[b])
        chain.append(a * moved + (1.0 - a) * chain[b])

    drain(zbuf.at[pl.ds(0, n_z - 1)], z_sem.at[1])
    z2 = zbuf.reshape(n_z * 24, LANES)
    def spread_rows(b):
        for r in range(4):
            tiles_s[BATCH_TILE + 4 * (b - 1) + r] = z2[pl.ds(BASE_ROW[b] + r, n_z, stride=24), :]
        mine = tiles_s.at[pl.ds(BATCH_TILE + 4 * (b - 1), 4)]
        for d in range(1, n_y):
            send(mine, gath.at[b - 1, my_col], y_sem.at[b - 1], zz * n_col + ((yy + d) % n_y) * n_core + core, lev)
        gath[b - 1, my_col] = tiles_s[BATCH_TILE + 4 * (b - 1) : BATCH_TILE + 4 * b]

    def cross_rows(b):
        drain(gath.at[b - 1, pl.ds(0, n_y - 1)], y_sem.at[b - 1, 1])
        mine = gath.at[b - 1, pl.ds(core * n_y, n_y)]
        send(mine, mine, g_sem.at[b - 1], me + 1 - 2 * core, lev)

    spread_rows(1)
    for g in range(n_lev):
        a = z2[pl.ds((g // 2) * 2, n_z, stride=24), :]
        c = z2[pl.ds((g // 2) * 2 + 1, n_z, stride=24), :]
        tiles_s[g] = jnp.where(low8, a, pltpu.roll(c, count, 1)) if g % 2 == 0 else jnp.where(low8, pltpu.roll(a, count, 1), c)
    for e in range(n_lev):
        level = (lev + e) % n_lev
        for d in range(n_col):
            if d or e:
                send(tiles_s.at[level], first.at[lev * n_col + my_col], f_sem, col_peer(d), level)
    first[lev * n_col + my_col] = tiles_s[lev]

    z_of_row = iota((n_z, LANES), 0)
    rows_of = [z2[pl.ds(4 + i, n_z, stride=24), :] for i in range(NB - 1)]
    found = [
        jnp.sum(jnp.where(z_of_row * n_col + yy * n_core + core == owner[b], rows_of[i], 0.0), axis=0, keepdims=True)
        for b, i in PAIRS
    ]
    tiles_s[n_lev] = jnp.concatenate(found + found[:2], axis=0)
    for d in range(1, n_col):
        send(tiles_s.at[n_lev], picks.at[my_col], p_sem, col_peer(d), lev)
    picks[my_col] = tiles_s[n_lev]
    spread_rows(2)
    spread_rows(3)

    def push_in(t, carry):
        peer = (me + t * 27) % n_grid
        send(
            x.at[:, pl.ds(pl.multiple_of(peer * rows, rows), rows), :],
            f.at[pl.ds(my_slot * slab, slab)],
            in_sem, peer, lev,
        )
        return carry

    def push_blocks(k):
        lax.fori_loop(CUTS[k], CUTS[k + 1], push_in, 0)

    push_blocks(0)
    f[pl.ds(my_slot * slab, slab)] = x[:, pl.ds(pl.multiple_of(me * rows, rows), rows), :]

    low_half = iota((half, LANES), 1) < count
    shift = {b: jnp.zeros((1, n_lev * count), F32) for b in range(1, NB)}

    def exchange_base(b, v):
        top, bottom = v[:half], v[half:]
        for g in range(n_lev):
            lanes = slice((g // 2) * LANES, (g // 2 + 1) * LANES)
            a, c = top[:, lanes], bottom[:, lanes]
            if g % 2 == 0:
                packed = jnp.where(low_half, a, pltpu.roll(c, count, 1))
            else:
                packed = jnp.where(low_half, pltpu.roll(a, count, 1), c)
            ssend[b - 1, g] = packed
        for d in range(1, n_lev):
            level = (lev + d) % n_lev
            send(ssend.at[b - 1, level], srecv.at[b - 1, d - 1], s_sem.at[b - 1], me, level)

    def member_values(b):
        parts = []
        for h in range(2):
            two = [gath[b - 1, :, h * 2 + i].reshape(n_grid, LANES) for i in range(slab)]
            parts.append(jnp.concatenate(two, axis=0))
        return jnp.concatenate(parts, axis=1)

    def base(b, v, pair_cols):
        for i in range(b):
            ys[PAIRS.index((b, i))] = v
            a = alpha[i, b]
            v = a * pick_dot(picker(pair_cols, PAIRS.index((b, i))), v) + (1.0 - a) * v
        exchange_base(b, v)

    def weigh(b, prior):
        seen = jnp.concatenate([val[b], val[b]], axis=1)
        dev = jnp.concatenate([err[b], err[b]], axis=1)
        innovation = ((seen - prior) / dev) ** 2
        changes = {}
        for key in list(range(b + 1, NB)) + [0]:
            weighted = innovation * taper[b, key]
            top = jnp.sum(jnp.where(low_half, weighted, 0.0), axis=1, keepdims=True)
            bottom = jnp.sum(jnp.where(low_half, 0.0, weighted), axis=1, keepdims=True)
            log_weight = (-0.5 / count) * jnp.concatenate([top, bottom], axis=0)
            expo = jnp.exp(log_weight - jnp.max(log_weight, axis=0, keepdims=True))
            changes[key] = expo / jnp.sum(expo, axis=0, keepdims=True) - 1.0 / members
        return changes

    def move(b, change, v):
        shift[b] = shift[b] + jnp.sum(change * v, axis=0, keepdims=True)

    def push_shift(b):
        for g in range(n_lev):
            row = shift[b][:, (g // 2) * LANES : (g // 2 + 1) * LANES]
            other = pltpu.roll(row, count, 1)
            left = lane1 < count
            row = jnp.where(left, row, other) if g % 2 == 0 else jnp.where(left, other, row)
            csend[b - 1, g] = jnp.broadcast_to(row, (8, LANES))
        for d in range(1, n_lev):
            level = (lev + d) % n_lev
            send(csend.at[b - 1, level], crecv.at[b - 1, d - 1], r_sem.at[b - 1], me, level)

    def full_prior(b):
        drain(srecv.at[b - 1], s_sem.at[b - 1, 1])
        prior = ssend[b - 1, lev]
        for d in range(n_lev - 1):
            prior = prior + srecv[b - 1, d]
        drain(crecv.at[b - 1], r_sem.at[b - 1, 1])
        row = csend[b - 1, lev]
        for d in range(n_lev - 1):
            row = row + crecv[b - 1, d]
        return prior + row[0:1, :]

    for b in range(1, NB):
        cross_rows(b)
    drain(first.at[pl.ds(0, n_lev * n_col - 1)], f_sem.at[1])
    prior = first[:n_col]
    for level in range(1, n_lev):
        prior = prior + first[level * n_col : (level + 1) * n_col]
    change = {0: weigh(0, prior.reshape(half, LANES))}
    push_blocks(1)

    drain(picks.at[pl.ds(0, n_col - 1)], p_sem.at[1])
    chosen = picks[0]
    for k in range(1, n_col):
        chosen = chosen + picks[k]
    pair_cols = columns(chosen)
    for b in range(1, NB):
        drain(gath.at[b - 1, pl.ds(0, n_y)], g_sem.at[b - 1, 1])
        v = member_values(b)
        if b == 1:
            move(1, change[0][1], v)
            base(1, v, pair_cols)
            push_shift(1)
            push_blocks(2)
        else:
            base(b, v, pair_cols)
            move(b, change[0][b], v)
    push_blocks(3)
    for b in range(1, NB):
        change[b] = weigh(b, full_prior(b))
        for later in range(b + 1, NB):
            move(later, change[b][later], ys[PAIRS.index((later, b))])
            if later == b + 1:
                push_shift(later)
        push_blocks(3 + b)
    mean_row = jnp.zeros((1, members), F32)
    for b in range(NB):
        mean_row = mean_row + jnp.sum(change[b][0] * chain[b], axis=0, keepdims=True)

    total = chain[NB] + mean_row
    t_hi, t_mid, _ = split3(total)
    drain(f.at[pl.ds(0, members - slab)], in_sem.at[1])
    f2 = f.reshape(members * rows, LANES)
    y2 = y.reshape(members * rows, LANES)
    for s in range(rows):
        two = [f2[pl.ds(i * rows + s, n_grid, stride=slab * rows), :] for i in range(slab)]
        hi, mid, _ = split3(jnp.concatenate(two, axis=0))
        mixed = (dot(t_mid, hi) + dot(t_hi, mid)) + dot(t_hi, hi)
        for i in range(slab):
            y2[pl.ds(i * rows + s, n_grid, stride=slab * rows), :] = mixed[i * n_grid : (i + 1) * n_grid]

    def push_out(t, carry):
        peer = (me + t) % n_grid
        send(
            y.at[pl.ds(slot_of(peer) * slab, slab)],
            out.at[:, pl.ds(pl.multiple_of(me * rows, rows), rows), :],
            out_sem, peer, lev,
        )
        return carry

    lax.fori_loop(1, n_grid, push_out, 0)
    out[:, pl.ds(pl.multiple_of(me * rows, rows), rows), :] = y[pl.ds(my_slot * slab, slab)]

    drain(zbuf.at[pl.ds(0, n_z - 1)], z_sem.at[0])
    drain(first.at[pl.ds(0, n_lev * n_col - 1)], f_sem.at[0])
    drain(picks.at[pl.ds(0, n_col - 1)], p_sem.at[0])
    for b in range(NB - 1):
        drain(gath.at[b, pl.ds(0, n_y - 1)], y_sem.at[b, 0])
        drain(gath.at[b, pl.ds(0, n_y)], g_sem.at[b, 0])
    drain(f.at[pl.ds(0, members - slab)], in_sem.at[0])
    for b in range(NB - 1):
        drain(srecv.at[b], s_sem.at[b, 0])
        drain(crecv.at[b], r_sem.at[b, 0])
    drain(y.at[pl.ds(0, members - slab)], out_sem.at[1])
    drain(y.at[pl.ds(0, members - slab)], out_sem.at[0])


def body(n_grid, n_lev, prior_fields, channel_weights, obs_owner, obs_offset, obs_value, obs_error, ancestors):
    slab, depth, cells = prior_fields.shape
    tiles = cells // LANES
    x = prior_fields.reshape(slab, depth, tiles, LANES).transpose(0, 2, 1, 3).reshape(slab, tiles * depth, LANES)
    members = slab * n_grid
    rows = tiles * depth // n_grid
    count = obs_offset.shape[2]
    n_col = 8
    n_z = n_grid // n_col
    vm = pl.BlockSpec(memory_space=pltpu.VMEM)
    hbm = pl.BlockSpec(memory_space=pltpu.HBM)
    pair = pltpu.SemaphoreType.DMA((2,))
    arrays = (obs_owner, channel_weights, x, obs_offset, obs_value, obs_error, ancestors.reshape(NB, 1, members))
    out = pl.pallas_call(
        functools.partial(kernel, n_grid, n_lev),
        out_shape=jax.ShapeDtypeStruct((slab, tiles * depth, LANES), F32),
        in_specs=[hbm] * 7,
        out_specs=vm,
        scratch_shapes=[
            pltpu.SMEM(obs_owner.shape, jnp.int32),
            pltpu.SMEM(channel_weights.shape, F32),
            pltpu.VMEM(x.shape, F32),
            pltpu.VMEM(obs_offset.shape, jnp.int32),
            pltpu.VMEM(obs_value.shape, F32),
            pltpu.VMEM(obs_error.shape, F32),
            pltpu.VMEM((NB, 1, members), jnp.int32),
            pltpu.VMEM((24, LANES), F32),
            pltpu.VMEM((n_z, 24, LANES), F32),
            pltpu.VMEM((n_lev * n_col, n_z, LANES), F32),
            pltpu.VMEM((n_col, 8, LANES), F32),
            pltpu.VMEM((NB - 1, n_col, 4, n_z, LANES), F32),
            pltpu.VMEM((members, rows, LANES), F32),
            pltpu.VMEM((members, rows, LANES), F32),
            pltpu.VMEM((len(PAIRS), members, n_lev * count), F32),
            pltpu.VMEM((NB - 1, n_lev, members // 2, LANES), F32),
            pltpu.VMEM((NB - 1, n_lev - 1, members // 2, LANES), F32),
            pltpu.VMEM((NB - 1, n_lev, 8, LANES), F32),
            pltpu.VMEM((NB - 1, n_lev - 1, 8, LANES), F32),
            pltpu.VMEM((BATCH_TILE + 4 * (NB - 1), 8, LANES), F32),
            pltpu.SemaphoreType.DMA((7,)),
            pair, pair, pair,
            pltpu.SemaphoreType.DMA((NB - 1, 2)),
            pltpu.SemaphoreType.DMA((NB - 1, 2)),
            pair, pair,
            pltpu.SemaphoreType.DMA((NB - 1, 2)),
            pltpu.SemaphoreType.DMA((NB - 1, 2)),
        ],
        compiler_params=pltpu.CompilerParams(
            has_side_effects=True, collective_id=0, vmem_limit_bytes=24 * 1024 * 1024
        ),
    )(*[pltpu.with_memory_space_constraint(v, pltpu.HBM) for v in arrays])
    return out.reshape(slab, tiles, depth, LANES).transpose(0, 2, 1, 3).reshape(slab, depth, cells)


def solution(mesh):
    in_specs = (
        P("grid", "lev", None),
        P("lev", None),
        P(),
        P(),
        P(None, "lev", None),
        P(None, "lev", None),
        P(None, "lev", "grid", None),
    )
    out_specs = P("grid", "lev", None)
    step = functools.partial(body, mesh.shape["grid"], mesh.shape["lev"])
    return jax.shard_map(step, mesh=mesh, in_specs=in_specs, out_specs=out_specs, check_vma=False)
```

```python
import functools

import jax
import jax.numpy as jnp
from jax import lax
from jax.experimental import pallas as pl
from jax.experimental.pallas import tpu as pltpu
from jax.sharding import PartitionSpec as P

NB = 4
LANES = 128
F32 = jnp.float32
BF16 = jnp.bfloat16
MESH = pl.DeviceIdType.MESH
BASE_ROW = (0, 8, 12, 16)
BATCH_TILE = 5
CUTS = (1, 64, 64, 64, 64, 64, 64, 64)
PAIRS = [(1, 0), (2, 0), (2, 1), (3, 0), (3, 1), (3, 2)]


def iota(shape, axis):
    return lax.broadcasted_iota(jnp.int32, shape, axis)


def split3(v):
    hi = v.astype(BF16)
    rest = v - hi.astype(F32)
    mid = rest.astype(BF16)
    low = (rest - mid.astype(F32)).astype(BF16)
    return hi, mid, low


def dot(a, b):
    return jnp.dot(a, b, preferred_element_type=F32)


def pick_dot(onehot, v):
    hi, mid, low = split3(v)
    return (dot(onehot, low) + dot(onehot, mid)) + dot(onehot, hi)


def kernel(
    n_grid, n_lev, owner_h, cw_h, x_h, off_h, val_h, err_h, anc_h, out,
    owner, cw, x, off, val, err, anc, pay, zbuf, first, picks, gath, f, y, ys, ssend, srecv, csend, crecv, tiles_s,
    load_sem, z_sem, f_sem, p_sem, y_sem, g_sem, in_sem, out_sem, s_sem, r_sem,
):
    slab = x.shape[0]
    rows = x.shape[1] // n_grid
    members = slab * n_grid
    half = members // 2
    count = off.shape[2]
    block = rows * LANES // 2
    n_core, n_y = 2, 4
    n_z = n_grid // (n_core * n_y)
    n_col = n_core * n_y
    scale = n_grid / 2.0

    me = lax.axis_index("grid")
    lev = lax.axis_index("lev")
    core = me % n_core
    yy = (me // n_core) % n_y
    zz = me // n_col

    def slot_of(g):
        return (g % n_core) * (n_y * n_z) + ((g // n_core) % n_y) * n_z + g // n_col

    def grid_of(s):
        return ((s % n_z) * n_y + (s // n_z) % n_y) * n_core + s // (n_z * n_y)

    my_slot = slot_of(me)
    my_col = core * n_y + yy

    def col_peer(d):
        return zz * n_col + (me + d) % n_col

    loads = []
    for k, (src, dst) in enumerate(
        [(x_h, x), (owner_h, owner), (off_h, off), (cw_h, cw), (anc_h, anc), (val_h, val), (err_h, err)]
    ):
        copy = pltpu.make_async_copy(src, dst, load_sem.at[k])
        copy.start()
        loads.append(copy)

    barrier = pltpu.get_barrier_semaphore()

    def hello(grid, level):
        pl.semaphore_signal(barrier, inc=1, device_id=(grid, level), device_id_type=MESH)

    for d in range(1, n_z):
        hello((me + d * n_col) % n_grid, lev)
    for e in range(n_lev):
        for d in range(n_col):
            if d or e:
                hello(col_peer(d), (lev + e) % n_lev)

    def send(src, dst, sem, grid, level):
        pltpu.make_async_remote_copy(
            src_ref=src, dst_ref=dst, send_sem=sem.at[0], recv_sem=sem.at[1],
            device_id=(grid, level), device_id_type=MESH,
        ).start()

    def drain(ref, sem):
        pltpu.make_async_copy(ref, ref, sem).wait()

    for copy in loads:
        copy.wait()

    lane256 = iota((1, n_lev * count), 1)
    wrow = []
    for level in range(2):
        w = jnp.zeros((1, n_lev * count), F32)
        for g in range(n_lev):
            w = jnp.where(lane256 // count == g, cw[level, g], w)
        wrow.append(w)
    row16 = iota((slab * rows, n_lev * count), 0)
    weights = jnp.where(row16 % 2 == 0, wrow[0], wrow[1])
    tile_of_row = (row16 % rows) // 2

    def scan_blocks(k, tiles):
        tile = x[:, pl.ds(pl.multiple_of(k * rows, rows), rows), :]
        return tuple(jnp.where(owner[b] == k, tile, kept) for b, kept in enumerate(tiles))

    zero = jnp.zeros((slab, rows, LANES), F32)
    tiles = lax.fori_loop(0, n_grid, scan_blocks, (zero,) * NB, unroll=8)
    pay[...] = jnp.zeros_like(pay)
    for b in range(NB):
        src = tiles[b].reshape(slab * rows, LANES)
        cells = jnp.concatenate([off[b, g : g + 1, :] for g in range(n_lev)], axis=1)
        onehot = (iota((LANES, n_lev * count), 0) == cells % LANES).astype(BF16)
        hi, mid, low = split3(src)
        got = (dot(low, onehot) + dot(mid, onehot)) + dot(hi, onehot)
        got = jnp.where(tile_of_row == cells // LANES, got * weights, 0.0)
        for i in range(slab):
            value = jnp.sum(got[i * rows : (i + 1) * rows], axis=0, keepdims=True)
            for h in range(2):
                at = BASE_ROW[b] + h * 2 + i
                pay[at : at + 1, :] = value[:, h * LANES : (h + 1) * LANES]
        if b < NB - 1:
            pay[4 + b : 5 + b, :] = anc[b].astype(F32)

    pl.semaphore_wait(barrier, n_z - 1 + n_lev * n_col - 1)

    for d in range(1, n_z):
        send(pay, zbuf.at[zz], z_sem, (me + d * n_col) % n_grid, lev)
    zbuf[zz] = pay[...]

    lane1 = iota((1, LANES), 1)
    low8 = iota((n_z, LANES), 1) < count
    member_lane = iota((members, members), 1)
    eye = (iota((members, members), 0) == member_lane).astype(F32)

    taper = {}
    alpha = {}
    for b in range(NB):
        cells = off[b, pl.ds(lev, 1), :]
        where = (owner[b] * block + cells).astype(F32) / block
        where = jnp.concatenate([where, where], axis=1)
        regions = {0: me}
        for later in range(b + 1, NB):
            regions[later] = owner[later]
        for key, region in regions.items():
            distance = ((region.astype(F32) + 0.5) - where) / scale
            t = jnp.exp(-0.5 * distance * distance)
            taper[b, key] = t
            total = jnp.sum(t, axis=1, keepdims=True)
            alpha[b, key] = 0.8 * (1.0 - jnp.exp(-total / (2 * count)))

    sub = iota((members, members), 0)
    perm = (grid_of(sub % n_grid) * slab + sub // n_grid == member_lane).astype(BF16)

    def columns(stack):
        stack = stack.astype(jnp.int32)
        stack = (slot_of(stack // slab) + (stack % slab) * n_grid).astype(F32).astype(BF16)
        return lax.dot_general(perm, stack, (((1,), (1,)), ((), ())), preferred_element_type=F32)

    def picker(cols, k):
        return (cols[:, k : k + 1].astype(jnp.int32) == member_lane).astype(BF16)

    own = [anc[b].astype(F32) for b in range(NB)]
    own_cols = columns(jnp.concatenate(own + own, axis=0))
    chain = [eye]
    for b in range(NB):
        a = alpha[b, 0]
        chosen = picker(own_cols, b)
        moved = chosen.astype(F32) if b == 0 else pick_dot(chosen, chain[b])
        chain.append(a * moved + (1.0 - a) * chain[b])

    drain(zbuf.at[pl.ds(0, n_z - 1)], z_sem.at[1])
    z2 = zbuf.reshape(n_z * 24, LANES)
    def spread_rows(b):
        for r in range(4):
            tiles_s[BATCH_TILE + 4 * (b - 1) + r] = z2[pl.ds(BASE_ROW[b] + r, n_z, stride=24), :]
        mine = tiles_s.at[pl.ds(BATCH_TILE + 4 * (b - 1), 4)]
        for d in range(1, n_y):
            send(mine, gath.at[b - 1, my_col], y_sem.at[b - 1], zz * n_col + ((yy + d) % n_y) * n_core + core, lev)
        gath[b - 1, my_col] = tiles_s[BATCH_TILE + 4 * (b - 1) : BATCH_TILE + 4 * b]

    def cross_rows(b):
        drain(gath.at[b - 1, pl.ds(0, n_y - 1)], y_sem.at[b - 1, 1])
        mine = gath.at[b - 1, pl.ds(core * n_y, n_y)]
        send(mine, mine, g_sem.at[b - 1], me + 1 - 2 * core, lev)

    spread_rows(1)
    z_of_row = iota((n_z, LANES), 0)
    rows_of = [z2[pl.ds(4 + i, n_z, stride=24), :] for i in range(NB - 1)]
    found = [
        jnp.sum(jnp.where(z_of_row * n_col + yy * n_core + core == owner[b], rows_of[i], 0.0), axis=0, keepdims=True)
        for b, i in PAIRS
    ]
    tiles_s[n_lev] = jnp.concatenate(found + found[:2], axis=0)
    for d in range(1, n_col):
        send(tiles_s.at[n_lev], picks.at[my_col], p_sem, col_peer(d), lev)
    picks[my_col] = tiles_s[n_lev]
    for g in range(n_lev):
        a = z2[pl.ds((g // 2) * 2, n_z, stride=24), :]
        c = z2[pl.ds((g // 2) * 2 + 1, n_z, stride=24), :]
        tiles_s[g] = jnp.where(low8, a, pltpu.roll(c, count, 1)) if g % 2 == 0 else jnp.where(low8, pltpu.roll(a, count, 1), c)
    for e in range(n_lev):
        level = (lev + e) % n_lev
        for d in range(n_col):
            if d or e:
                send(tiles_s.at[level], first.at[lev * n_col + my_col], f_sem, col_peer(d), level)
    first[lev * n_col + my_col] = tiles_s[lev]

    spread_rows(2)
    spread_rows(3)

    def push_in(t, carry):
        peer = (me + t * 27) % n_grid
        send(
            x.at[:, pl.ds(pl.multiple_of(peer * rows, rows), rows), :],
            f.at[pl.ds(my_slot * slab, slab)],
            in_sem, peer, lev,
        )
        return carry

    def push_blocks(k):
        lax.fori_loop(CUTS[k], CUTS[k + 1], push_in, 0)

    push_blocks(0)
    f[pl.ds(my_slot * slab, slab)] = x[:, pl.ds(pl.multiple_of(me * rows, rows), rows), :]

    low_half = iota((half, LANES), 1) < count
    shift = {b: jnp.zeros((1, n_lev * count), F32) for b in range(1, NB)}

    def exchange_base(b, v):
        top, bottom = v[:half], v[half:]
        for g in range(n_lev):
            lanes = slice((g // 2) * LANES, (g // 2 + 1) * LANES)
            a, c = top[:, lanes], bottom[:, lanes]
            if g % 2 == 0:
                packed = jnp.where(low_half, a, pltpu.roll(c, count, 1))
            else:
                packed = jnp.where(low_half, pltpu.roll(a, count, 1), c)
            ssend[b - 1, g] = packed
        for d in range(1, n_lev):
            level = (lev + d) % n_lev
            send(ssend.at[b - 1, level], srecv.at[b - 1, d - 1], s_sem.at[b - 1], me, level)

    def member_values(b):
        parts = []
        for h in range(2):
            two = [gath[b - 1, :, h * 2 + i].reshape(n_grid, LANES) for i in range(slab)]
            parts.append(jnp.concatenate(two, axis=0))
        return jnp.concatenate(parts, axis=1)

    def base(b, v, pair_cols):
        for i in range(b):
            ys[PAIRS.index((b, i))] = v
            a = alpha[i, b]
            v = a * pick_dot(picker(pair_cols, PAIRS.index((b, i))), v) + (1.0 - a) * v
        exchange_base(b, v)

    def weigh(b, prior):
        seen = jnp.concatenate([val[b], val[b]], axis=1)
        dev = jnp.concatenate([err[b], err[b]], axis=1)
        innovation = ((seen - prior) / dev) ** 2
        changes = {}
        for key in list(range(b + 1, NB)) + [0]:
            weighted = innovation * taper[b, key]
            top = jnp.sum(jnp.where(low_half, weighted, 0.0), axis=1, keepdims=True)
            bottom = jnp.sum(jnp.where(low_half, 0.0, weighted), axis=1, keepdims=True)
            log_weight = (-0.5 / count) * jnp.concatenate([top, bottom], axis=0)
            expo = jnp.exp(log_weight - jnp.max(log_weight, axis=0, keepdims=True))
            changes[key] = expo / jnp.sum(expo, axis=0, keepdims=True) - 1.0 / members
        return changes

    def move(b, change, v):
        shift[b] = shift[b] + jnp.sum(change * v, axis=0, keepdims=True)

    def push_shift(b):
        for g in range(n_lev):
            row = shift[b][:, (g // 2) * LANES : (g // 2 + 1) * LANES]
            other = pltpu.roll(row, count, 1)
            left = lane1 < count
            row = jnp.where(left, row, other) if g % 2 == 0 else jnp.where(left, other, row)
            csend[b - 1, g] = jnp.broadcast_to(row, (8, LANES))
        for d in range(1, n_lev):
            level = (lev + d) % n_lev
            send(csend.at[b - 1, level], crecv.at[b - 1, d - 1], r_sem.at[b - 1], me, level)

    def full_prior(b):
        drain(srecv.at[b - 1], s_sem.at[b - 1, 1])
        prior = ssend[b - 1, lev]
        for d in range(n_lev - 1):
            prior = prior + srecv[b - 1, d]
        drain(crecv.at[b - 1], r_sem.at[b - 1, 1])
        row = csend[b - 1, lev]
        for d in range(n_lev - 1):
            row = row + crecv[b - 1, d]
        return prior + row[0:1, :]

    for b in range(1, NB):
        cross_rows(b)
    drain(first.at[pl.ds(0, n_lev * n_col - 1)], f_sem.at[1])
    prior = first[:n_col]
    for level in range(1, n_lev):
        prior = prior + first[level * n_col : (level + 1) * n_col]
    change = {0: weigh(0, prior.reshape(half, LANES))}
    push_blocks(1)

    drain(picks.at[pl.ds(0, n_col - 1)], p_sem.at[1])
    chosen = picks[0]
    for k in range(1, n_col):
        chosen = chosen + picks[k]
    pair_cols = columns(chosen)
    for b in range(1, NB):
        drain(gath.at[b - 1, pl.ds(0, n_y)], g_sem.at[b - 1, 1])
        v = member_values(b)
        if b == 1:
            base(1, v, pair_cols)
            move(1, change[0][1], v)
            push_shift(1)
            push_blocks(2)
        else:
            base(b, v, pair_cols)
            move(b, change[0][b], v)
    push_blocks(3)
    for b in range(1, NB):
        change[b] = weigh(b, full_prior(b))
        for later in range(b + 1, NB):
            move(later, change[b][later], ys[PAIRS.index((later, b))])
            if later == b + 1:
                push_shift(later)
        push_blocks(3 + b)
    mean_row = jnp.zeros((1, members), F32)
    for b in range(NB):
        mean_row = mean_row + jnp.sum(change[b][0] * chain[b], axis=0, keepdims=True)

    total = chain[NB] + mean_row
    t_hi, t_mid, _ = split3(total)
    drain(f.at[pl.ds(0, members - slab)], in_sem.at[1])
    f2 = f.reshape(members * rows, LANES)
    y2 = y.reshape(members * rows, LANES)
    for s in range(rows):
        two = [f2[pl.ds(i * rows + s, n_grid, stride=slab * rows), :] for i in range(slab)]
        hi, mid, _ = split3(jnp.concatenate(two, axis=0))
        mixed = (dot(t_mid, hi) + dot(t_hi, mid)) + dot(t_hi, hi)
        for i in range(slab):
            y2[pl.ds(i * rows + s, n_grid, stride=slab * rows), :] = mixed[i * n_grid : (i + 1) * n_grid]

    def push_out(t, carry):
        peer = (me + t) % n_grid
        send(
            y.at[pl.ds(slot_of(peer) * slab, slab)],
            out.at[:, pl.ds(pl.multiple_of(me * rows, rows), rows), :],
            out_sem, peer, lev,
        )
        return carry

    lax.fori_loop(1, n_grid, push_out, 0)
    out[:, pl.ds(pl.multiple_of(me * rows, rows), rows), :] = y[pl.ds(my_slot * slab, slab)]

    drain(zbuf.at[pl.ds(0, n_z - 1)], z_sem.at[0])
    drain(first.at[pl.ds(0, n_lev * n_col - 1)], f_sem.at[0])
    drain(picks.at[pl.ds(0, n_col - 1)], p_sem.at[0])
    for b in range(NB - 1):
        drain(gath.at[b, pl.ds(0, n_y - 1)], y_sem.at[b, 0])
        drain(gath.at[b, pl.ds(0, n_y)], g_sem.at[b, 0])
    drain(f.at[pl.ds(0, members - slab)], in_sem.at[0])
    for b in range(NB - 1):
        drain(srecv.at[b], s_sem.at[b, 0])
        drain(crecv.at[b], r_sem.at[b, 0])
    drain(y.at[pl.ds(0, members - slab)], out_sem.at[1])
    drain(y.at[pl.ds(0, members - slab)], out_sem.at[0])


def body(n_grid, n_lev, prior_fields, channel_weights, obs_owner, obs_offset, obs_value, obs_error, ancestors):
    slab, depth, cells = prior_fields.shape
    tiles = cells // LANES
    x = prior_fields.reshape(slab, depth, tiles, LANES).transpose(0, 2, 1, 3).reshape(slab, tiles * depth, LANES)
    members = slab * n_grid
    rows = tiles * depth // n_grid
    count = obs_offset.shape[2]
    n_col = 8
    n_z = n_grid // n_col
    vm = pl.BlockSpec(memory_space=pltpu.VMEM)
    hbm = pl.BlockSpec(memory_space=pltpu.HBM)
    pair = pltpu.SemaphoreType.DMA((2,))
    arrays = (obs_owner, channel_weights, x, obs_offset, obs_value, obs_error, ancestors.reshape(NB, 1, members))
    out = pl.pallas_call(
        functools.partial(kernel, n_grid, n_lev),
        out_shape=jax.ShapeDtypeStruct((slab, tiles * depth, LANES), F32),
        in_specs=[hbm] * 7,
        out_specs=vm,
        scratch_shapes=[
            pltpu.SMEM(obs_owner.shape, jnp.int32),
            pltpu.SMEM(channel_weights.shape, F32),
            pltpu.VMEM(x.shape, F32),
            pltpu.VMEM(obs_offset.shape, jnp.int32),
            pltpu.VMEM(obs_value.shape, F32),
            pltpu.VMEM(obs_error.shape, F32),
            pltpu.VMEM((NB, 1, members), jnp.int32),
            pltpu.VMEM((24, LANES), F32),
            pltpu.VMEM((n_z, 24, LANES), F32),
            pltpu.VMEM((n_lev * n_col, n_z, LANES), F32),
            pltpu.VMEM((n_col, 8, LANES), F32),
            pltpu.VMEM((NB - 1, n_col, 4, n_z, LANES), F32),
            pltpu.VMEM((members, rows, LANES), F32),
            pltpu.VMEM((members, rows, LANES), F32),
            pltpu.VMEM((len(PAIRS), members, n_lev * count), F32),
            pltpu.VMEM((NB - 1, n_lev, members // 2, LANES), F32),
            pltpu.VMEM((NB - 1, n_lev - 1, members // 2, LANES), F32),
            pltpu.VMEM((NB - 1, n_lev, 8, LANES), F32),
            pltpu.VMEM((NB - 1, n_lev - 1, 8, LANES), F32),
            pltpu.VMEM((BATCH_TILE + 4 * (NB - 1), 8, LANES), F32),
            pltpu.SemaphoreType.DMA((7,)),
            pair, pair, pair,
            pltpu.SemaphoreType.DMA((NB - 1, 2)),
            pltpu.SemaphoreType.DMA((NB - 1, 2)),
            pair, pair,
            pltpu.SemaphoreType.DMA((NB - 1, 2)),
            pltpu.SemaphoreType.DMA((NB - 1, 2)),
        ],
        compiler_params=pltpu.CompilerParams(
            has_side_effects=True, collective_id=0, vmem_limit_bytes=24 * 1024 * 1024
        ),
    )(*[pltpu.with_memory_space_constraint(v, pltpu.HBM) for v in arrays])
    return out.reshape(slab, tiles, depth, LANES).transpose(0, 2, 1, 3).reshape(slab, depth, cells)


def solution(mesh):
    in_specs = (
        P("grid", "lev", None),
        P("lev", None),
        P(),
        P(),
        P(None, "lev", None),
        P(None, "lev", None),
        P(None, "lev", "grid", None),
    )
    out_specs = P("grid", "lev", None)
    step = functools.partial(body, mesh.shape["grid"], mesh.shape["lev"])
    return jax.shard_map(step, mesh=mesh, in_specs=in_specs, out_specs=out_specs, check_vma=False)
```
